32 devices in a mesh: tok: 8 (over z, x), feat: 4 (over y, core).
Axes of the slice: x: 2, y: 2, z: 4, core: 2. Of those that a mesh axis runs over, the one named last changes fastest.
Arguments:
- activations: bfloat16 [8192, 28672], P('tok', 'feat'), may hold values from -6 to 6
- out_grads: bfloat16 [8192, 8192], P('tok', 'feat'), may hold values from -6 to 6
- proj_in: bfloat16 [28672, 256], P('feat'), may hold values from -0.03125 to 0.03125
- proj_out: bfloat16 [8192, 256], P('feat'), may hold values from -0.0625 to 0.0625
- left_factor: float32 [256, 256], replicated, may hold values from -0.375 to 0.375
- right_factor: float32 [256, 256], replicated, may hold values from -0.375 to 0.375
- seq_lengths: int32 [64], replicated, may hold values from 1 to 255, as said below
- seq_slots: int32 [64], replicated, may hold values from 0 to 63, each once
- stored_grads: float32 [256, 65536], P('tok', 'feat'), may hold values from -0.375 to 0.375
Outputs:
- scores: float32 [256, 64], P(('tok', 'feat'))
- seq_grads: float32 [64, 65536], P('tok', 'feat')
The draws below stay inside these ranges and needn't reach their ends.
Inputs may be any that keep to these rules, and one draw needn't show every extreme that they name: `seq_lengths`: the lengths sum to 8192. Sequence s starts within tokens s * (128) to (s + 1) * 128 - 1, the first at token 0, so exactly 8 sequences start in the tokens of each index of tok, at most 9 sequences meet them (exactly that many at index 1), and a sequence meets the tokens of at most two indices. The longest is exactly 255. `seq_slots`: every slot is used by exactly one sequence.
All inputs are finite; a program needn't handle non-finite values.
Results may differ from the reference program's by a relative error of at most 0.0003.
Values sent between devices are 32-bit elements; how exact they have to be, the bound alone decides.
A program may use at most 128 MiB of HBM per device.

```python
import jax
import jax.numpy as jnp
from jax import lax

D_IN = 28672
D_OUT = 8192
K = 256
TOK_DEV = 1024
SEQ_DEV = 8
TOKENS = 8192
SEQS = 64
STORE = 256
MOST_LEN = 255


def draw_seq_lengths(key, part):
    spacing = TOK_DEV // SEQ_DEV
    jitter = jax.random.randint(jax.random.fold_in(key, 7), (SEQS,), 0, spacing).astype(jnp.int32)
    jitter = jitter.at[0].set(0)
    jitter = jitter.at[SEQ_DEV - 1].set(0)
    jitter = jitter.at[SEQ_DEV].set(spacing - 1)
    starts = jnp.arange(SEQS, dtype=jnp.int32) * spacing + jitter
    ends = jnp.concatenate([starts[1:], jnp.full((1,), TOKENS, jnp.int32)])
    return (ends - starts).astype(jnp.int32)


def levels(stream_key, dims, cuts, low, largest):
    factor_of, own = 1.0, jax.random.fold_in(stream_key, 6)
    for position, blocks in cuts:
        steps = jnp.exp(jax.random.uniform(jax.random.fold_in(own, position), (blocks,), jnp.float32, low / len(cuts), largest / len(cuts)))
        factor_of = factor_of * jnp.repeat(steps, dims[position] // blocks).reshape([-1 if axis == position else 1 for axis in range(len(dims))])
    return factor_of


def normal_values(stream_key, shape, spread, bound, cuts=(), held_as=jnp.bfloat16):
    level = levels(stream_key, shape, cuts, -0.22, 0.18) if cuts else 1.0
    entries = jax.random.normal(stream_key, shape, jnp.float32) * spread * level
    return jnp.minimum(jnp.maximum(entries, -bound), bound).astype(held_as)


def setup_inputs(seed: int = 0) -> dict:
    splits = jax.random.split(jax.random.key(seed), 10)
    return {
        "activations": normal_values(splits[0], (TOKENS, D_IN), 1.0, 6.0, ((0, 8), (1, 4))),
        "out_grads": normal_values(splits[1], (TOKENS, D_OUT), 1.0, 6.0, ((0, 8), (1, 4))),
        "proj_in": normal_values(splits[2], (D_IN, K), D_IN ** -0.5, 0.03125, ((0, 4),)),
        "proj_out": normal_values(splits[3], (D_OUT, K), D_OUT ** -0.5, 0.0625, ((0, 4),)),
        "left_factor": normal_values(splits[4], (K, K), K ** -0.5, 0.375, (), jnp.float32),
        "right_factor": normal_values(splits[5], (K, K), K ** -0.5, 0.375, (), jnp.float32),
        "seq_lengths": draw_seq_lengths(jax.random.fold_in(splits[9], 71), 0),
        "seq_slots": jax.random.permutation(splits[7], SEQS).astype(jnp.int32),
        "stored_grads": normal_values(splits[8], (STORE, K * K), (16.0 / K), 0.375, ((0, 8), (1, 4)), jnp.float32),
    }


def reference(activations, out_grads, proj_in, proj_out, left_factor, right_factor, seq_lengths, seq_slots, stored_grads):
    in_proj = jnp.dot(activations, proj_in, preferred_element_type=jnp.float32)
    out_proj = jnp.dot(out_grads, proj_out, preferred_element_type=jnp.float32)
    right_side = jnp.dot(in_proj, right_factor, precision=lax.Precision.HIGHEST)
    left_side = jnp.dot(out_proj, left_factor.T, precision=lax.Precision.HIGHEST)
    ends = jnp.cumsum(seq_lengths).astype(jnp.int32)
    starts = (ends - seq_lengths).astype(jnp.int32)

    def one_sequence(pair):
        start, length = pair
        first = jnp.clip(start, 0, TOKENS - MOST_LEN).astype(jnp.int32)
        left_win = lax.dynamic_slice_in_dim(left_side, first, MOST_LEN, 0)
        right_win = lax.dynamic_slice_in_dim(right_side, first, MOST_LEN, 0)
        places = first + jnp.arange(MOST_LEN, dtype=jnp.int32)
        inside = ((places >= start) & (places < start + length)).astype(jnp.float32)
        weights = inside / length.astype(jnp.float32)
        weighted = weights[:, None] * left_win
        return jnp.dot(weighted.T, right_win, precision=lax.Precision.HIGHEST).reshape(K * K)

    per_sequence = lax.map(one_sequence, (starts, seq_lengths))
    seq_grads = jnp.zeros((SEQS, K * K), jnp.float32).at[seq_slots].set(per_sequence)
    scores = jnp.dot(stored_grads, seq_grads.T, precision=lax.Precision.HIGHEST)
    return scores, seq_grads
```

```python
import functools

import jax
import jax.numpy as jnp
from jax import lax
from jax.experimental import pallas as pl
from jax.experimental.pallas import tpu as pltpu
from jax.sharding import PartitionSpec as P

MESH = pl.DeviceIdType.MESH
VMEM = pl.BlockSpec(memory_space=pltpu.VMEM)
ANY = pl.BlockSpec(memory_space=pl.ANY)
F32, BF16 = jnp.float32, jnp.bfloat16
DOWN, UP = 0, 1


def halves(value):
    high = value.astype(BF16)
    return high, (value - high.astype(F32)).astype(BF16)


def times(left, right):
    return jnp.dot(left, right, preferred_element_type=F32)


def times_t(left, right):
    return lax.dot_general(left, right, (((1,), (1,)), ((), ())), preferred_element_type=F32)


def stack_left(value, axis):
    high, low = halves(value)
    return jnp.concatenate([high, low, high], axis=axis)


def stack_right(value, axis):
    high, low = halves(value)
    return jnp.concatenate([high, high, low], axis=axis)


def aligned(index, size):
    return pl.ds(pl.multiple_of(index * size, size), size)


def kernel(dims, *refs):
    toks, feats, local, chunk, rank, seqs, store_rows = dims
    out_rows, in_rows, out_mat, in_mat, left_hbm, right_hbm, lens_hbm, slots_hbm, stored = refs[:9]
    total, out = refs[9:11]
    lhs_o, lhs_i, rhs_o, rhs_i, left_f, right_f, lens, slots = refs[11:19]
    left_cat, right_cat = refs[19:21]
    lp, la, ly, lb, lfin = refs[21:26]
    rp, ra, ry, rb, rfull = refs[26:31]
    block, hx, hz, gs = refs[31:35]
    kept, given, mats, sc, picked, scored, landed = refs[35:42]
    load, asem, bsem, csem, xsem, hsem, zsend, zrecv, ssem, psem, rsem = refs[42:]

    tok, feat = lax.axis_index("tok"), lax.axis_index("feat")
    plane, x = tok // 2, tok % 2
    y, c = feat // 2, feat % 2
    planes = toks // 2
    mate, chips = feat + 1 - 2 * c, feats // 2
    across = [(y + turn) % chips for turn in range(1, chips)]
    beside = tok + 1 - 2 * x
    wide = rank // feats
    half_o = wide // 2
    quarters = half_o // 8
    in_plane = 2 * local
    half_lanes = half_o * rank
    part_lanes = 8 * rank
    tiles = rank // 128
    below, above = plane > 0, plane < planes - 1

    def remote(src, dst, sems, to_tok, to_feat):
        return pltpu.make_async_remote_copy(
            src_ref=src, dst_ref=dst, send_sem=sems[0], recv_sem=sems[1],
            device_id=(to_tok, to_feat), device_id_type=MESH,
        )

    small = [(left_hbm, left_f), (right_hbm, right_f), (lens_hbm, lens), (slots_hbm, slots)]
    loads = {}

    def fetch(key, src, dst):
        loads[key] = pltpu.make_async_copy(src, dst, load.at[len(loads)])
        loads[key].start()

    fetch("out", out_mat, rhs_o)
    fetch(("o", 0), out_rows.at[pl.ds(0, chunk)], lhs_o.at[0])
    fetch("left", *small[0])
    fetch("in", in_mat, rhs_i)
    fetch(("i", 0), in_rows.at[pl.ds(0, chunk)], lhs_i.at[0])
    for n, name in ((1, "right"), (2, "lens"), (3, "slots")):
        fetch(name, *small[n])
    for k in range(1, local):
        fetch(("o", k), out_rows.at[pl.ds(k * chunk, chunk)], lhs_o.at[k])
        fetch(("i", k), in_rows.at[pl.ds(k * chunk, chunk)], lhs_i.at[k])
    fetch("kept", stored.at[:, aligned(x, half_lanes)], kept)

    barrier = pltpu.get_barrier_semaphore()

    def greet(to_tok, to_feat):
        pl.semaphore_signal(barrier, inc=1, device_id=(to_tok, to_feat), device_id_type=MESH)

    for step in range(2):
        for turn in range(feats):
            if step or turn:
                greet(beside if step else tok, (feat + turn) % feats)
    neighbours = [
        (below, tok - 2), (above, tok + 2),
        (below & (x == 0), tok - 1), (above & (x == 1), tok + 1),
    ]
    met = 2 * feats - 1
    for there, other in neighbours:
        met += there.astype(jnp.int32)

        @pl.when(there)
        def _():
            greet(other, feat)

    sent = []

    def start(copy):
        copy.start()
        sent.append(copy)
        return copy

    pieces = given.shape[1] // (2 * rank)
    trades = []

    def trade(count):
        for _ in range(count):
            n = len(trades)
            if n < pieces:
                lanes = pl.ds(n * 2 * rank, 2 * rank)
                first = pl.multiple_of((1 - x) * half_lanes + n * 2 * rank, 2 * rank)
                trades.append(start(remote(
                    stored.at[:, pl.ds(first, 2 * rank)], given.at[:, lanes],
                    (ssem.at[0, n], ssem.at[1, n]), beside, feat,
                )))

    copies = {}

    def project_out(k):
        loads["o", k].wait()
        if k == 0:
            loads["out"].wait()
        sums = times(lhs_o[k], rhs_o[...])
        if k == 0:
            loads["left"].wait()
            for core in range(2):
                for side in range(chips):
                    rows = left_f[pl.ds((side * 2 + core) * wide, wide), :]
                    left_cat[pl.ds((core * chips + side) * wide, wide), :] = stack_left(rows, 1)
        lp[k] = times_t(left_cat[...], stack_right(sums, 1)).reshape(2, chips, wide, chunk)
        if k == 0:
            pl.semaphore_wait(barrier, met)
            trade(3)
        copies["a", 0, k] = start(remote(
            lp.at[k, 1 - c], la.at[k], (asem.at[0, 0, k], asem.at[1, 0, k]), tok, mate))

    def pair_left(k):
        copies["a", 0, k].wait_recv()
        ly[k] = lp[k, c] + la[k]
        for n, other in enumerate(across):
            copies["b", 0, k, n] = start(remote(
                ly.at[k, other], lb.at[k, n], (bsem.at[0, 0, k, n], bsem.at[1, 0, k, n]),
                tok, other * 2 + c))

    def project_in(k):
        if k == 0:
            loads["in"].wait()
        loads["i", k].wait()
        depth = lhs_i.shape[2]
        cut = depth // 2
        sums = times(lhs_i[k, :, :cut], rhs_i[:cut, :])
        rp[k] = sums.reshape(2, chunk // 2, rank)
        pair_left(k)
        sums = times(lhs_i[k, :, cut:], rhs_i[cut:, :])
        rp[k] += sums.reshape(2, chunk // 2, rank)
        copies["a", 1, k] = start(remote(
            rp.at[k, 1 - c], ra.at[k], (asem.at[0, 1, k], asem.at[1, 1, k]), tok, mate))

    def pair_right(k):
        copies["a", 1, k].wait_recv()
        ry[k] = rp[k, c] + ra[k]
        for n, other in enumerate(across):
            copies["b", 1, k, n] = start(remote(
                ry.at[k], rb.at[k, n], (bsem.at[0, 1, k, n], bsem.at[1, 1, k, n]),
                tok, other * 2 + c))

    def finish_rows(k):
        if k == 0:
            loads["right"].wait()
            right_cat[...] = stack_right(right_f[...], 0)
        left, rows = ly[k, y], ry[k]
        for n in range(chips - 1):
            copies["b", 0, k, n].wait_recv()
            left += lb[k, n]
        lfin[k] = left
        for n in range(chips - 1):
            copies["b", 1, k, n].wait_recv()
            rows += rb[k, n]
        rfull[k, c] = times(stack_left(rows, 1), right_cat[...])
        copies["c", k] = start(remote(
            rfull.at[k, c], rfull.at[k, c], (csem.at[0, k], csem.at[1, k]), tok, mate))

    spans = {}

    def starts_of():
        loads["lens"].wait()
        lengths = lens[...].astype(F32)
        number = lax.broadcasted_iota(jnp.int32, (local, seqs), 1)
        mine = lax.broadcasted_iota(jnp.int32, (local, seqs), 0) + tok * local

        def pick(mask):
            return jnp.sum(jnp.where(mask, lengths, 0.0), axis=1, keepdims=True)

        spans["start"] = pick(number < mine)
        spans["now"] = 1.0 / jnp.maximum(pick(number == mine), 1.0)
        spans["before"] = 1.0 / jnp.maximum(pick(number == mine - 1), 1.0)

    def seq_rows(at_plane, number, side, count=1):
        first = (at_plane * in_plane + number * 2 + side) * 8
        return pl.ds(pl.multiple_of(first, 8), 8 * count)

    def settle(k, value):
        for tile in range(tiles):
            part = value[:, tile * 128 : (tile + 1) * 128]
            block[k, :, :, tile] = part.reshape(2, quarters, 8, 128)
        if k < local:
            gs[:, :, seq_rows(plane, k, x), :] = block[k, x]
            copies["x", k] = start(remote(
                block.at[k, 1 - x], gs.at[:, :, seq_rows(plane, k, x), :],
                (xsem.at[0, k], xsem.at[1, k]), beside, feat))

    def head_copies():
        return (
            (x == 1, remote(block.at[local, 0], hx, (hsem.at[0, 0], hsem.at[1, 0]), beside, feat)),
            ((x == 0) & below, remote(
                block.at[local, 0], hz, (hsem.at[0, 1], hsem.at[1, 1]), tok - 2, feat)),
            ((x == 0) & below, remote(
                block.at[local, 1], hz, (hsem.at[0, 2], hsem.at[1, 1]), tok - 1, feat)),
        )

    carry = {}

    def gradients(k):
        if k == 0:
            starts_of()
        copies["c", k].wait_recv()
        places = lax.broadcasted_iota(jnp.int32, (1, chunk), 1) + (tok * local + k) * chunk
        inside = places.astype(F32) >= spans["start"][k : k + 1]
        now = jnp.where(inside, spans["now"][k : k + 1], 0.0)
        before = jnp.where(inside, 0.0, spans["before"][k : k + 1])
        left = lfin[k]
        weighted = jnp.concatenate([left * now, left * before], axis=0)
        right = rfull[k].reshape(chunk, rank)
        both = times(stack_left(weighted, 1), stack_right(right, 0))
        tail = both[wide:]
        if k:
            settle(k - 1, carry["sum"] + tail)
        else:
            settle(local, tail)
            for when, copy in head_copies():
                pl.when(when)(copy.start)
        carry["sum"] = both[:wide]
        if k == local - 1:
            settle(k, carry["sum"])

    ways = (DOWN, UP)

    def block_plane(way, step):
        return jnp.clip(plane + step if way == DOWN else plane - step, 0, planes - 1)

    def sending(way, step):
        if way == DOWN:
            return below & (plane + step < planes)
        return above & (plane - step >= 0)

    def taking(way, step):
        return plane + 1 + step < planes if way == DOWN else plane - 1 - step >= 0

    def parts_of(step):
        return local if step == 0 else local // 2 if step == 1 else quarters

    def z_copy(way, step, part):
        at = block_plane(way, step)
        if step < 2:
            count = 1 if step == 0 else 2
            piece = gs.at[:, :, seq_rows(at, part * count, 0, 2 * count), :]
        else:
            piece = gs.at[part, :, seq_rows(at, 0, 0, in_plane), :]
        return remote(
            piece, piece, (zsend.at[way, step, part], zrecv.at[way, step, part]),
            tok - 2 if way == DOWN else tok + 2, feat,
        )

    def z_each(way, step, part, what, when):
        @pl.when(when)
        def _():
            getattr(z_copy(way, step, part), what)()

    last_step = max(planes - 2, 0)

    def complete(k):
        copies["x", k].wait_recv()
        if k == local - 1:
            @pl.when(x == 1)
            def _():
                gs[:, :, seq_rows(plane, k, 0), :] += block[local, 1]

            @pl.when(x == 0)
            def _():
                head_copies()[0][1].wait_recv()
                gs[:, :, seq_rows(plane, k, 0), :] += hx[...]

            @pl.when(above)
            def _():
                head_copies()[1][1].wait_recv()
                gs[:, :, seq_rows(plane, k, 1), :] += hz[...]
        if planes > 1:
            for way in ways:
                z_each(way, 0, k, "start", sending(way, 0))

    def take(step, parts, onward):
        if step > last_step or planes < 2:
            return
        for part in parts:
            for way in ways:
                z_each(way, step, part, "wait_recv", taking(way, step))
        if step < last_step:
            for part in onward:
                for way in ways:
                    z_each(way, step + 1, part, "start", sending(way, step + 1))

    def make_mats(rows, lanes, value):
        high, low = halves(value)
        count = 2 * store_rows
        mats[pl.ds(rows * store_rows, store_rows), lanes] = high
        mats[pl.ds(count + rows * store_rows, store_rows), lanes] = low

    def score(at, part):
        lines = []
        for line in range(8):
            first = at * in_plane * 8 + line
            for tile in range(tiles):
                lines.append(gs[part, tile, pl.ds(first, in_plane, stride=8), :])
        high, low = halves(jnp.concatenate(lines, axis=1))
        return times_t(
            jnp.concatenate([high, low], axis=0),
            mats[:, pl.ds(part * part_lanes, part_lanes)],
        )

    def score_plane(at):
        value = score(at, 0)
        for part in range(1, quarters):
            value += score(at, part)
        sc[at] = value

    def score_step(step):
        for way in ways:
            @pl.when(taking(way, step))
            def _():
                score_plane(block_plane(way, step + 1))

    def stage_rows(k):
        if 0 <= k < local:
            finish_rows(k)

    def stage_grads(k):
        if 0 <= k < local:
            gradients(k)
            trade(1)

    def stage_complete(k):
        if 0 <= k < local:
            complete(k)
            group = k // 2 - 1
            if k % 2 == 0 and group >= 0:
                take(0, (2 * group, 2 * group + 1), (group,))

    rows_done, grads_done = 0, 0
    for k in range(local):
        project_out(k)
        if k:
            pair_right(k - 1)
        project_in(k)
        if 0 < k < 4:
            trade(1)
        if k >= 2 and k % 2 == 0:
            stage_rows(rows_done)
            rows_done += 1
        elif k >= 3:
            stage_grads(grads_done)
            grads_done += 1
            stage_complete(grads_done - 3)
    pair_right(local - 1)
    while grads_done < local:
        if rows_done == grads_done:
            stage_rows(rows_done)
            rows_done += 1
        stage_complete(grads_done - 2)
        stage_grads(grads_done)
        grads_done += 1
    trade(pieces)
    stage_complete(local - 2)
    loads["kept"].wait()
    make_mats(0, pl.ds(0, half_lanes), kept[...])
    stage_complete(local - 1)

    loads["slots"].wait()
    at_row = lax.broadcasted_iota(jnp.int32, (seqs, seqs), 1)
    seq_of = ((at_row // in_plane) * 2 + at_row % 2) * local + (at_row % in_plane) // 2
    order = jnp.where(lax.broadcasted_iota(jnp.int32, (seqs, seqs), 0) == seq_of, 1.0, 0.0)
    slot = lax.broadcasted_iota(jnp.int32, (seqs, seqs), 0)
    by_slot = times(
        jnp.where(slots[...] == slot, 1.0, 0.0).astype(BF16), order.astype(BF16))
    row = lax.broadcasted_iota(jnp.int32, (2 * local, seqs), 0)
    wanted = jnp.where(row < local, tok * local + row, beside * local + row - local)
    pick = times(
        jnp.where(slots[...] == wanted, 1.0, 0.0).astype(BF16), order.astype(BF16)).astype(BF16)
    pick = jnp.concatenate([pick, pick], axis=1)

    groups = local // 2
    for copy in trades:
        copy.wait_recv()
    make_mats(1, pl.ds(0, half_lanes), given[...])
    take(0, (local - 2, local - 1), (groups - 1,))
    score_plane(plane)
    if last_step > 0:
        score_step(0)
        take(1, range(groups), range(quarters))
        if last_step > 1:
            score_step(1)
        for step in range(2, last_step):
            take(step, range(quarters), range(quarters))
            score_step(step)

    def rows_for_slots(part):
        for line in range(8):
            high, low = halves(jnp.concatenate(
                [gs[part, tile, pl.ds(line, seqs, stride=8), :] for tile in range(tiles)], axis=1))
            taken = times(pick, jnp.concatenate([high, low], axis=0))
            lane = part * part_lanes + line * rank
            out[:, pl.ds(pl.multiple_of(x * half_lanes + lane, rank), rank)] = taken[:local]
            picked[:, pl.ds(lane, rank)] = taken[local:]
        there = pl.ds(pl.multiple_of(x * half_lanes + part * part_lanes, part_lanes), part_lanes)
        copies["p", part] = start(remote(
            picked.at[:, pl.ds(part * part_lanes, part_lanes)], out.at[:, there],
            (psem.at[0, part], psem.at[1, part]), beside, feat))

    by_part = last_step >= 2
    for part in range(quarters):
        if by_part:
            take(last_step, (part,), ())
        rows_for_slots(part)
    if planes > 1:
        score_step(last_step)

    count = 2 * store_rows
    sums = sc[...]
    high_high, high_low, low_high = sums[:, :in_plane], sums[:, :in_plane], sums[:, in_plane:]
    by_row = (
        high_high[:, :, :count] + high_low[:, :, count:] + low_high[:, :, :count]
    ).reshape(seqs, count)
    few = scored.shape[2]
    lanes = scored.shape[3]
    placed = jnp.dot(by_slot, by_row, precision=lax.Precision.HIGHEST, preferred_element_type=F32)
    square = jnp.zeros((lanes, 128 - count), F32)
    tall = jnp.zeros((lanes - seqs, count), F32)
    if lanes > seqs:
        placed = jnp.concatenate([placed, tall], axis=0)
    turned = jnp.transpose(jnp.concatenate([placed, square], axis=1))
    for step in range(2):
        for f in range(feats):
            first = (step * feats + f) * few
            scored[step, f] = turned[first : first + few]
    parts = []
    for step in range(2):
        for turn in range(feats):
            if step or turn:
                to = (feat + turn) % feats
                parts.append(start(remote(
                    scored.at[step, to], landed.at[step, turn],
                    (rsem.at[0, step, turn], rsem.at[1, step, turn]),
                    beside if step else tok, to,
                )))
    summed = scored[0, feat]
    for number, copy in enumerate(parts, 1):
        copy.wait_recv()
        summed += landed[number // feats, number % feats]
    total[...] = summed[:, :seqs]

    for part in range(quarters):
        copies["p", part].wait_recv()
    for copy in sent:
        copy.wait_send()
    for when, copy in head_copies():
        pl.when(when)(copy.wait_send)
    if planes > 1:
        for step in range(last_step + 1):
            for way in ways:
                for part in range(parts_of(step)):
                    z_each(way, step, part, "wait_send", sending(way, step))


def body(
    activations,
    out_grads,
    proj_in,
    proj_out,
    left_factor,
    right_factor,
    seq_lengths,
    seq_slots,
    stored_grads,
):
    dma = pltpu.SemaphoreType.DMA
    feats, toks = lax.axis_size("feat"), lax.axis_size("tok")
    rank = right_factor.shape[0]
    tok_rows = activations.shape[0]
    seqs = seq_lengths.shape[0]
    local = seqs // toks
    chunk = tok_rows // local
    store_rows, width = stored_grads.shape
    planes, chips = toks // 2, feats // 2
    wide = rank // feats
    quarters = wide // 16
    tiles = rank // 128
    score_rows = store_rows // feats
    lanes = seqs + -seqs % 128
    half = chunk // 2
    steps = max(planes - 1, 1)
    pieces = width // 2 // (2 * rank)

    def vmem(*shape, dtype=F32):
        return pltpu.VMEM(shape, dtype)

    scores, own_rows = pl.pallas_call(
        functools.partial(kernel, (toks, feats, local, chunk, rank, seqs, store_rows)),
        out_shape=[
            jax.ShapeDtypeStruct((score_rows, seqs), F32),
            jax.ShapeDtypeStruct((local, width), F32),
        ],
        in_specs=[ANY] * 9,
        out_specs=[VMEM] * 2,
        scratch_shapes=[
            vmem(local, chunk, out_grads.shape[1], dtype=BF16),
            vmem(local, chunk, activations.shape[1], dtype=BF16),
            vmem(*proj_out.shape, dtype=BF16),
            vmem(*proj_in.shape, dtype=BF16),
            vmem(rank, rank),
            vmem(rank, rank),
            vmem(1, seqs, dtype=jnp.int32),
            vmem(1, seqs, dtype=jnp.int32),
            vmem(rank, 3 * rank, dtype=BF16),
            vmem(3 * rank, rank, dtype=BF16),
            vmem(local, 2, chips, wide, chunk),
            vmem(local, chips, wide, chunk),
            vmem(local, chips, wide, chunk),
            vmem(local, chips - 1, wide, chunk),
            vmem(local, wide, chunk),
            vmem(local, 2, half, rank),
            vmem(local, half, rank),
            vmem(local, half, rank),
            vmem(local, chips - 1, half, rank),
            vmem(local, 2, half, rank),
            vmem(local + 1, 2, quarters, tiles, 8, 128),
            vmem(quarters, tiles, 8, 128),
            vmem(quarters, tiles, 8, 128),
            vmem(quarters, tiles, seqs * 8, 128),
            vmem(store_rows, width // 2),
            vmem(store_rows, width // 2),
            vmem(4 * store_rows, width // 2, dtype=BF16),
            vmem(planes, 4 * local, 4 * store_rows),
            vmem(local, width // 2),
            vmem(2, feats, score_rows, lanes),
            vmem(2, feats, score_rows, lanes),
            dma((2 * local + 7,)),
            dma((2, 2, local)),
            dma((2, 2, local, chips - 1)),
            dma((2, local)),
            dma((2, local)),
            dma((2, 3)),
            dma((2, steps, local)),
            dma((2, steps, local)),
            dma((2, pieces)),
            dma((2, quarters)),
            dma((2, 2, feats)),
        ],
        compiler_params=pltpu.CompilerParams(
            collective_id=0, has_side_effects=True, vmem_limit_bytes=60 << 20
        ),
        name="influence",
    )(
        out_grads, activations, proj_out, proj_in, left_factor, right_factor,
        seq_lengths.reshape(1, seqs), seq_slots.reshape(1, seqs), stored_grads,
    )
    return scores, own_rows


def solution(mesh):
    placed = (
        P("tok", "feat"),
        P("tok", "feat"),
        P("feat", None),
        P("feat", None),
        P(),
        P(),
        P(),
        P(),
        P("tok", "feat"),
    )
    return jax.shard_map(
        body,
        mesh=mesh,
        in_specs=placed,
        out_specs=(P(("tok", "feat"), None), P("tok", "feat")),
        check_vma=False,
    )
```

```python
import functools

import jax
import jax.numpy as jnp
from jax import lax
from jax.experimental import pallas as pl
from jax.experimental.pallas import tpu as pltpu
from jax.sharding import PartitionSpec as P

MESH = pl.DeviceIdType.MESH
VMEM = pl.BlockSpec(memory_space=pltpu.VMEM)
ANY = pl.BlockSpec(memory_space=pl.ANY)
F32, BF16 = jnp.float32, jnp.bfloat16
DOWN, UP = 0, 1


def halves(value):
    high = value.astype(BF16)
    return high, (value - high.astype(F32)).astype(BF16)


def times(left, right):
    return jnp.dot(left, right, preferred_element_type=F32)


def times_t(left, right):
    return lax.dot_general(left, right, (((1,), (1,)), ((), ())), preferred_element_type=F32)


def stack_left(value, axis):
    high, low = halves(value)
    return jnp.concatenate([high, low, high], axis=axis)


def stack_right(value, axis):
    high, low = halves(value)
    return jnp.concatenate([high, high, low], axis=axis)


def aligned(index, size):
    return pl.ds(pl.multiple_of(index * size, size), size)


def pushed_quarters(planes, quarters):
    return quarters // 4 if planes == 4 else 0


def both(first, second):
    if first is True:
        return second
    if second is True:
        return first
    return False if first is False or second is False else first & second


def no(value):
    return not value if isinstance(value, bool) else jnp.logical_not(value)


def when(condition, action):
    if condition is True:
        action()
    elif condition is not False:
        pl.when(condition)(action)


def kernel(dims, *refs):
    toks, feats, local, chunk, rank, seqs, store_rows = dims
    out_rows, in_rows, out_mat, in_mat, left_hbm, right_hbm, lens_hbm, slots_hbm, stored = refs[:9]
    total, out = refs[9:11]
    lhs_o, lhs_i, rhs_o, rhs_i, left_f, right_f, lens, slots = refs[11:19]
    left_cat, right_cat, folded = refs[19:22]
    lp, la, ly, lb, lfin = refs[22:27]
    rp, ra, ry, rb, rfull = refs[27:32]
    block, hx, hz, gs = refs[32:36]
    kept, given, guest, mats, guest_mats, sc, guest_sc = refs[36:43]
    found, picked, scored, landed = refs[43:47]
    load, asem, bsem, csem, xsem, hsem, zrecv, zrecv_late, srecv, precv, rrecv = refs[47:58]
    asent, bsent, csent, xsent, hsent, zsent, ssent, psent, rsent, wsent = refs[58:]

    tok, feat = lax.axis_index("tok"), lax.axis_index("feat")
    plane, x = tok // 2, tok % 2
    y, c = feat // 2, feat % 2
    planes = toks // 2
    mate, chips = feat + 1 - 2 * c, feats // 2
    across = [(y + turn) % chips for turn in range(1, chips)]
    beside = tok + 1 - 2 * x
    wide = rank // feats
    half_o = wide // 2
    quarters = half_o // 8
    in_plane = 2 * local
    half_lanes = half_o * rank
    part_lanes = 8 * rank
    tiles = rank // 128
    below, above = plane > 0, plane < planes - 1
    pushed = pushed_quarters(planes, quarters)
    outer = inner = False
    if pushed:
        outer = (plane == 0) | (plane == planes - 1)
        inner = (plane == 1) | (plane == planes - 2)
    partner = jnp.where(plane == 0, 1, jnp.where(
        plane == planes - 1, planes - 2, jnp.where(plane == 1, 0, planes - 1)))

    def remote(src, dst, sems, to_tok, to_feat):
        return pltpu.make_async_remote_copy(
            src_ref=src, dst_ref=dst, send_sem=sems[0], recv_sem=sems[1],
            device_id=(to_tok, to_feat), device_id_type=MESH,
        )

    loads = {}
    span = 2 if local % 2 == 0 else 1
    blocks = local // span
    tall = span * chunk

    def fetch(key, src, dst):
        loads[key] = pltpu.make_async_copy(src, dst, load.at[len(loads)])
        loads[key].start()

    def fetch_block(b):
        if b < blocks:
            rows = pl.ds(b * tall, tall)
            fetch(("i", b), in_rows.at[rows], lhs_i.at[rows])
            fetch(("o", b), out_rows.at[rows], lhs_o.at[rows])

    fetch("left", left_hbm, left_f)
    fetch("out", out_mat, rhs_o)
    fetch("in", in_mat, rhs_i)
    fetch_block(0)
    fetch("lens", lens_hbm, lens)
    fetch("slots", slots_hbm, slots)
    fetch("right", right_hbm, right_f)

    barrier = pltpu.get_barrier_semaphore()

    def greet(to_tok, to_feat):
        pl.semaphore_signal(barrier, inc=1, device_id=(to_tok, to_feat), device_id_type=MESH)

    for step in range(2):
        for turn in range(feats):
            if step or turn:
                greet(beside if step else tok, (feat + turn) % feats)
    met = 2 * feats - 1
    for side, there, crossing in ((-1, below, 0), (1, above, 1)):
        near = False
        if pushed:
            near = (outer & (partner == plane + side)) | (inner & (partner == plane + side))
        plain = both(there, no(near))
        corner = both(plain, x == crossing)
        met += plain.astype(jnp.int32) + corner.astype(jnp.int32)

        def greet_all(side=side):
            for other in range(2):
                for f in range(feats):
                    greet((plane + side) * 2 + other, f)

        if pushed:
            met += 2 * feats * near.astype(jnp.int32)
        when(near, greet_all)
        when(plain, lambda side=side: greet(tok + 2 * side, feat))
        when(corner, lambda side=side: greet(tok + side, feat))

    sent = []

    def start(copy, condition=True):
        when(condition, copy.start)
        return copy

    def await_sent(src, sem, condition=True):
        copy = remote(src, src, (sem, sem), tok, mate)
        sent.append((condition, copy))

    def await_all(dst, sem, condition=True):
        copy = remote(dst, dst, (sem, sem), tok, mate)
        when(condition, copy.wait_recv)

    piece = 2 * rank
    pieces = half_lanes // piece
    aside = pushed * part_lanes // piece
    trades = []

    def column(half, first, count=1):
        lanes = half * half_lanes + first * piece
        return pl.ds(pl.multiple_of(lanes, piece), piece * count)

    def push_own():
        copy = remote(
            stored.at[:, column(x, 0, aside)], guest.at[0], (ssent.at[2], srecv.at[2]),
            partner * 2 + x, feat)
        start(copy, outer)
        await_sent(stored.at[:, column(x, 0, aside)], ssent.at[2], outer)

    def push_given():
        lanes = pl.ds(0, aside * piece)
        await_all(given.at[:, lanes], srecv.at[0], outer)
        copy = remote(
            given.at[:, lanes], guest.at[1], (ssent.at[3], srecv.at[3]), partner * 2 + x, feat)
        start(copy, outer)
        await_sent(given.at[:, lanes], ssent.at[3], outer)

    def trade(count):
        for _ in range(count):
            n = len(trades)
            if n < pieces:
                kind = 0 if n < aside else 1
                trades.append(start(remote(
                    stored.at[:, column(1 - x, n)], given.at[:, pl.ds(n * piece, piece)],
                    (ssent.at[kind], srecv.at[kind]), beside, feat,
                )))

    def trades_sent():
        if aside:
            await_sent(stored.at[:, column(1 - x, 0, aside)], ssent.at[0])
        await_sent(stored.at[:, column(1 - x, aside, pieces - aside)], ssent.at[1])

    copies = {}

    def fold_left():
        loads["left"].wait()
        for core in range(2):
            for side in range(chips):
                rows = left_f[pl.ds((side * 2 + core) * wide, wide), :]
                high, low = halves(rows)
                left_cat[0, pl.ds((core * chips + side) * wide, wide), :] = high
                left_cat[1, pl.ds((core * chips + side) * wide, wide), :] = low
        loads["out"].wait()
        depth = rhs_o.shape[0]
        step = min(256, depth)
        for n in range(depth // step):
            rows = rhs_o[pl.ds(n * step, step), :]
            folded[0, pl.ds(n * step, step), :], folded[1, pl.ds(n * step, step), :] = halves(
                times_t(rows, left_cat[0]) + times_t(rows, left_cat[1]))

    def project_out(b):
        loads["o", b].wait()
        own = [lhs_o[pl.ds((b * span + n) * chunk, chunk), :] for n in range(span)]
        sums = [times(rows, folded[0]) + times(rows, folded[1]) for rows in own]
        for n in range(span):
            lp[b * span + n] = jnp.transpose(sums[n]).reshape(2, chips, wide, chunk)

    def send_left(b):
        for k in range(b * span, b * span + span):
            copies["a", 0, k] = start(remote(
                lp.at[k, 1 - c], la.at[k], (asent.at[0], asem.at[0, k]), tok, mate))

    def pair_left(k):
        copies["a", 0, k].wait_recv()
        ly[k] = lp[k, c] + la[k]
        for n, other in enumerate(across):
            copies["b", 0, k, n] = start(remote(
                ly.at[k, other], lb.at[k, n], (bsent.at[0, n], bsem.at[0, k, n]),
                tok, other * 2 + c))

    def project_in(b):
        if b == 0:
            loads["in"].wait()
        loads["i", b].wait()
        fetch_block(b + 2)
        own = [lhs_i[pl.ds((b * span + n) * chunk, chunk), :] for n in range(span)]
        for n, sums in enumerate([times(rows, rhs_i[...]) for rows in own]):
            rp[b * span + n] = sums.reshape(2, chunk // 2, rank)

    def send_right(b):
        for k in range(b * span, b * span + span):
            copies["a", 1, k] = start(remote(
                rp.at[k, 1 - c], ra.at[k], (asent.at[1], asem.at[1, k]), tok, mate))

    def pair_right(k):
        copies["a", 1, k].wait_recv()
        ry[k] = rp[k, c] + ra[k]
        for n, other in enumerate(across):
            copies["b", 1, k, n] = start(remote(
                ry.at[k], rb.at[k, n], (bsent.at[1, n], bsem.at[1, k, n]),
                tok, other * 2 + c))

    def rows_sent():
        for side, ref in ((0, lp), (1, rp)):
            await_sent(ref.at[:, 1 - c], asent.at[side])
        for n, other in enumerate(across):
            await_sent(ly.at[:, other], bsent.at[0, n])
            await_sent(ry, bsent.at[1, n])
        await_sent(rfull.at[:, c], csent.at[0])
        await_sent(block.at[pl.ds(0, local), 1 - x], xsent.at[0])

    def finish_rows(k):
        if k == 0:
            loads["right"].wait()
            right_cat[...] = stack_right(right_f[...], 0)
        left, rows = ly[k, y], ry[k]
        for n in range(chips - 1):
            copies["b", 0, k, n].wait_recv()
            left += lb[k, n]
        lfin[k] = left
        for n in range(chips - 1):
            copies["b", 1, k, n].wait_recv()
            rows += rb[k, n]
        rfull[k, c] = times(stack_left(rows, 1), right_cat[...])
        copies["c", k] = start(remote(
            rfull.at[k, c], rfull.at[k, c], (csent.at[0], csem.at[k]), tok, mate))

    spans = {}

    def starts_of():
        loads["lens"].wait()
        lengths = lens[...].astype(F32)
        number = lax.broadcasted_iota(jnp.int32, (local, seqs), 1)
        mine = lax.broadcasted_iota(jnp.int32, (local, seqs), 0) + tok * local

        def pick(mask):
            return jnp.sum(jnp.where(mask, lengths, 0.0), axis=1, keepdims=True)

        spans["start"] = pick(number < mine)
        spans["now"] = 1.0 / jnp.maximum(pick(number == mine), 1.0)
        spans["before"] = 1.0 / jnp.maximum(pick(number == mine - 1), 1.0)

    def seq_rows(at_plane, number, side, count=1):
        first = (at_plane * in_plane + number * 2 + side) * 8
        return pl.ds(pl.multiple_of(first, 8), 8 * count)

    def settle(k, value):
        for tile in range(tiles):
            part = value[:, tile * 128 : (tile + 1) * 128]
            block[k, :, :, tile] = part.reshape(2, quarters, 8, 128)
        if k < local:
            gs[:, :, seq_rows(plane, k, x), :] = block[k, x]
            copies["x", k] = start(remote(
                block.at[k, 1 - x], gs.at[:, :, seq_rows(plane, k, x), :],
                (xsent.at[0], xsem.at[k]), beside, feat))

    def head_copies():
        return (
            (x == 1, remote(block.at[local, 0], hx, (hsent.at[0], hsem.at[0]), beside, feat)),
            ((x == 0) & below, remote(
                block.at[local, 0], hz, (hsent.at[1], hsem.at[1]), tok - 2, feat)),
            ((x == 0) & below, remote(
                block.at[local, 1], hz, (hsent.at[2], hsem.at[1]), tok - 1, feat)),
        )

    carry = {}

    def gradients(k):
        if k == 0:
            starts_of()
        copies["c", k].wait_recv()
        places = lax.broadcasted_iota(jnp.int32, (1, chunk), 1) + (tok * local + k) * chunk
        inside = places.astype(F32) >= spans["start"][k : k + 1]
        now = jnp.where(inside, spans["now"][k : k + 1], 0.0)
        before = jnp.where(inside, 0.0, spans["before"][k : k + 1])
        left = lfin[k]
        weighted = jnp.concatenate([left * now, left * before], axis=0)
        right = rfull[k].reshape(chunk, rank)
        both = times(stack_left(weighted, 1), stack_right(right, 0))
        tail = both[wide:]
        if k:
            settle(k - 1, carry["sum"] + tail)
        else:
            settle(local, tail)
            for condition, copy in head_copies():
                when(condition, copy.start)
        carry["sum"] = both[:wide]
        if k == local - 1:
            settle(k, carry["sum"])

    ways = (DOWN, UP)

    def block_plane(way, step):
        return jnp.clip(plane + step if way == DOWN else plane - step, 0, planes - 1)

    def to_outer(way):
        return (plane == 1 if way == DOWN else plane == planes - 2) if pushed else False

    def sending(way, step, kind=1):
        if way == DOWN:
            base = below & (plane + step < planes)
        else:
            base = above & (plane - step >= 0)
        return base if kind else both(base, no(to_outer(way)))

    def taking(way, step, kind=1):
        base = plane + 1 + step < planes if way == DOWN else plane - 1 - step >= 0
        return base if kind else both(base, no(outer))

    groups = local // 2
    tail_parts = range(pushed, quarters)
    kinds = (0, 1) if pushed else (1,)

    def z_data(at, step, kind, part, count):
        which = pl.ds(pushed, quarters - pushed) if kind else pl.ds(0, pushed)
        if step < 2:
            return gs.at[which, :, seq_rows(at, part, 0, 2 * count), :]
        return gs.at[part, :, seq_rows(at, 0, 0, in_plane), :]

    def z_sems(way, step, kind, part):
        came = zrecv.at[way, kind, part // 2] if step == 0 else (
            zrecv.at[way, kind, groups] if step == 1 else zrecv_late.at[way, step - 2, part])
        return zsent.at[way, kind, step], came

    def z_start(way, step, kind, part, condition):
        count = 2 if step == 1 else 1
        data = z_data(block_plane(way, step), step, kind, part * count, count)
        copy = remote(
            data, data, z_sems(way, step, kind, part),
            tok - 2 if way == DOWN else tok + 2, feat)
        when(condition, copy.start)

    def z_sent():
        for step in range(last_step + 1):
            for way in ways:
                for kind in kinds:
                    if step < 2:
                        data = z_data(block_plane(way, step), step, kind, 0, local)
                    else:
                        at = block_plane(way, step)
                        data = gs.at[pl.ds(pushed, quarters - pushed), :, seq_rows(at, 0, 0, in_plane), :]
                    if step < 2 or kind:
                        await_sent(data, zsent.at[way, kind, step], sending(way, step, kind))

    last_step = max(planes - 2, 0)

    def complete(k):
        copies["x", k].wait_recv()
        if k == local - 1:
            @pl.when(x == 1)
            def _():
                gs[:, :, seq_rows(plane, k, 0), :] += block[local, 1]

            @pl.when(x == 0)
            def _():
                head_copies()[0][1].wait_recv()
                gs[:, :, seq_rows(plane, k, 0), :] += hx[...]

            @pl.when(above)
            def _():
                head_copies()[1][1].wait_recv()
                gs[:, :, seq_rows(plane, k, 1), :] += hz[...]
        if planes > 1:
            for kind in kinds:
                for way in ways:
                    z_start(way, 0, kind, k, sending(way, 0, kind))

    def take(step, kind, part=0):
        if step <= last_step and planes > 1 and kind in kinds:
            for way in ways:
                first, count = (2 * part, 2) if step == 0 else (0, local)
                at = block_plane(way, step + 1)
                data = z_data(at, step, kind, first if step < 2 else part, count)
                came = z_sems(way, step, kind, first if step < 2 else part)[1]
                await_all(data, came, taking(way, step, kind))

    def forward(step, kind, parts, outermost=None):
        if step <= last_step and kind in kinds:
            for part in parts:
                for way in ways:
                    condition = sending(way, step, kind)
                    if outermost is not None:
                        end = to_outer(way)
                        condition = both(condition, end if outermost else no(end))
                    z_start(way, step, kind, part, condition)

    def pass_on(group):
        for kind in kinds:
            take(0, kind, group)
        forward(1, 0, (group,))
        if pushed:
            forward(1, 1, (group,), True)
        else:
            forward(1, 1, (group,))

    def make_mats(target, rows, lanes, value):
        high, low = halves(value)
        count = 2 * store_rows
        target[pl.ds(rows * store_rows, store_rows), lanes] = high
        target[pl.ds(count + rows * store_rows, store_rows), lanes] = low

    def score(target, at, part):
        lines = []
        for line in range(8):
            first = at * in_plane * 8 + line
            for tile in range(tiles):
                lines.append(gs[part, tile, pl.ds(first, in_plane, stride=8), :])
        high, low = halves(jnp.concatenate(lines, axis=1))
        return times_t(
            jnp.concatenate([high, low], axis=0),
            target[:, pl.ds(part * part_lanes, part_lanes)],
        )

    def score_plane(at):
        value = score(mats, at, pushed)
        for part in range(pushed + 1, quarters):
            value += score(mats, at, part)
        sc[at] = value

        def more():
            value = score(mats, at, 0)
            for part in range(1, pushed):
                value += score(mats, at, part)
            sc[at] += value

        if pushed:
            when(no(outer), more)

    def score_guests():
        for step in range(2):
            await_all(guest.at[step], srecv.at[2 + step])
        lanes = pl.ds(0, pushed * part_lanes)
        for step in range(2):
            make_mats(guest_mats, step, lanes, guest[step])
        for at in range(planes):
            value = score(guest_mats, at, 0)
            for part in range(1, pushed):
                value += score(guest_mats, at, part)
            guest_sc[at] = value

    def score_step(step):
        for way in ways:
            when(taking(way, step), lambda way=way: score_plane(block_plane(way, step + 1)))

    def stage_rows(k):
        if 0 <= k < local:
            finish_rows(k)

    def stage_grads(k):
        if 0 <= k < local:
            gradients(k)
            trade(1)

    def stage_complete(k):
        if 0 <= k < local:
            complete(k)

    fold_left()
    fetch_block(1)
    project_in(0)
    pl.semaphore_wait(barrier, met)
    if pushed:
        push_own()
    trade(3)
    for b in range(blocks):
        first = b * span
        send_right(b)
        project_out(b)
        send_left(b)
        pair_right(first)
        if b + 1 < blocks:
            project_in(b + 1)
        else:
            fetch("kept", stored.at[:, column(x, 0, pieces)], kept)
            stage_rows(0)
        pair_left(first)
        for k in range(first + 1, first + span):
            pair_right(k)
            pair_left(k)
        trade(1)
    for k in range(local):
        if k:
            stage_rows(k)
        stage_complete(k - 3)
        if k >= 6 and k % 2 == 0:
            pass_on(k // 2 - 3)
        stage_grads(k)
        if k == 1 and pushed:
            push_given()
    trade(pieces)
    trades_sent()
    rows_sent()
    passed = max(local // 2 - 3, 0)
    loads["kept"].wait()
    make_mats(mats, 0, pl.ds(0, half_lanes), kept[...])
    stage_complete(local - 3)
    if passed < groups - 2:
        pass_on(passed)
        passed += 1
    stage_complete(local - 2)
    stage_complete(local - 1)

    loads["slots"].wait()
    at_row = lax.broadcasted_iota(jnp.int32, (seqs, seqs), 1)
    seq_of = ((at_row // in_plane) * 2 + at_row % 2) * local + (at_row % in_plane) // 2
    by_seq = jnp.where(lax.broadcasted_iota(jnp.int32, (seqs, seqs), 0) == seq_of, 1.0, 0.0)
    by_seq = by_seq.astype(BF16)
    slot = lax.broadcasted_iota(jnp.int32, (seqs, seqs), 0)
    by_slot = times(
        jnp.where(slots[...] == slot, 1.0, 0.0).astype(BF16), by_seq)
    row = lax.broadcasted_iota(jnp.int32, (4 * local, seqs), 0)
    wanted = jnp.zeros((4 * local, seqs), jnp.int32)
    for n, owner in enumerate((tok, beside, partner * 2 + x, partner * 2 + 1 - x)):
        here = (row >= n * local) & (row < (n + 1) * local)
        wanted = jnp.where(here, owner * local + row - n * local, wanted)
    pick = times(
        jnp.where(slots[...] == wanted, 1.0, 0.0).astype(BF16), by_seq).astype(BF16)
    pick = jnp.concatenate([pick, pick], axis=1)

    while passed < groups - 1:
        pass_on(passed)
        passed += 1
    if aside:
        await_all(given.at[:, pl.ds(0, aside * piece)], srecv.at[0], no(outer))
    await_all(given.at[:, pl.ds(aside * piece, (pieces - aside) * piece)], srecv.at[1])

    def given_mats(first, count):
        lanes = pl.ds(first * part_lanes, count * part_lanes)
        make_mats(mats, 1, lanes, given[:, lanes])

    given_mats(pushed, quarters - pushed)
    if pushed:
        when(no(outer), lambda: given_mats(0, pushed))
    score_plane(plane)
    pass_on(groups - 1)
    if pushed:
        forward(1, 1, range(groups), False)
    score_step(0)

    def write(half, part, condition=True):
        lanes = pl.ds(pl.multiple_of(half * half_lanes + part * part_lanes, part_lanes), part_lanes)
        copy = pltpu.make_async_copy(found.at[:, lanes], out.at[:, lanes], wsent.at[0])
        when(condition, copy.start)

    def give(part, n, to, condition):
        lane = part * part_lanes
        there = pl.ds(pl.multiple_of(x * half_lanes + lane, part_lanes), part_lanes)
        sem = psent.at[n, 0 if part < pushed else 1]
        copies["p", n, part] = start(remote(
            picked.at[n, :, pl.ds(lane, part_lanes)], found.at[:, there],
            (sem, precv.at[n, part]), to, feat), condition)

    def rows_for_slots(part):
        count = 4 if part < pushed else 2

        def fill():
            for line in range(8):
                high, low = halves(jnp.concatenate(
                    [gs[part, tile, pl.ds(line, seqs, stride=8), :] for tile in range(tiles)], axis=1))
                taken = times(pick[: count * local], jnp.concatenate([high, low], axis=0))
                lane = part * part_lanes + line * rank
                found[:, pl.ds(pl.multiple_of(x * half_lanes + lane, rank), rank)] = taken[:local]
                for n in range(1, count):
                    picked[n - 1, :, pl.ds(lane, rank)] = taken[n * local : (n + 1) * local]

        condition = no(outer) if part < pushed else True
        when(condition, fill)
        if part < pushed:
            give(part, 1, partner * 2 + x, inner)
            give(part, 2, partner * 2 + 1 - x, inner)
        give(part, 0, beside, condition)
        write(x, part, condition)

    if pushed:
        take(1, 0)
        for part in range(pushed):
            rows_for_slots(part)
    take(1, 1)
    forward(2, 1, tail_parts)
    if last_step > 0:
        score_step(1)
    for step in range(2, last_step):
        for part in tail_parts:
            take(step, 1, part)
        forward(step + 1, 1, tail_parts)
        score_step(step)
    if pushed:
        when(inner, score_guests)
    for part in tail_parts:
        if last_step >= 2:
            take(last_step, 1, part)
        rows_for_slots(part)
    if last_step >= 2:
        score_step(last_step)

    def turn_scores(sums):
        count = 2 * store_rows
        high, low = sums[:, :in_plane], sums[:, in_plane:]
        by_row = (high[:, :, :count] + high[:, :, count:] + low[:, :, :count]).reshape(seqs, count)
        lanes = scored.shape[4]
        placed = jnp.dot(
            by_slot, by_row, precision=lax.Precision.HIGHEST, preferred_element_type=F32)
        if lanes > seqs:
            placed = jnp.concatenate([placed, jnp.zeros((lanes - seqs, count), F32)], axis=0)
        return jnp.transpose(
            jnp.concatenate([placed, jnp.zeros((lanes, 128 - count), F32)], axis=1))

    few = scored.shape[3]
    parts = {}

    def send_scores(kind, own, condition):
        base = partner if kind else plane
        for step in range(2):
            for turn in range(feats):
                if kind or step or turn:
                    to = (feat + turn) % feats
                    parts[kind, step, turn] = start(remote(
                        scored.at[kind, step, to], landed.at[kind, step * feats + turn],
                        (rsent.at[kind], rrecv.at[kind]),
                        base * 2 + (1 - x if step else x), to,
                    ), condition)
        first = 0 if kind else 1
        await_sent(landed.at[kind, pl.ds(first, 2 * feats - first)], rsent.at[kind], condition)

    def place_scores(kind, sums):
        turned = turn_scores(sums)
        for step in range(2):
            for f in range(feats):
                first = (step * feats + f) * few
                scored[kind, step, f] = turned[first : first + few]

    def share_scores():
        if pushed:
            when(inner, lambda: place_scores(1, guest_sc[...]))
            send_scores(1, guest_sc, inner)
        place_scores(0, sc[...])
        send_scores(0, sc, True)

    def sum_scores():
        others = pl.ds(1, 2 * feats - 1)
        await_all(landed.at[0, others], rrecv.at[0])
        summed = scored[0, 0, feat]
        for n in range(1, 2 * feats):
            summed += landed[0, n]
        total[...] = summed[:, :seqs]

        def add_more():
            await_all(landed.at[1], rrecv.at[1])
            more = landed[1, 0]
            for n in range(1, 2 * feats):
                more += landed[1, n]
            total[...] += more[:, :seqs]

        if pushed:
            when(outer, add_more)

    def drain():
        for part in range(quarters):
            arrives = no(outer) if part < pushed else True
            when(arrives, copies["p", 0, part].wait_recv)
            write(1 - x, part, arrives)
        for part in range(pushed):
            for n, half in ((1, x), (2, 1 - x)):
                when(outer, copies["p", n, part].wait_recv)
                write(half, part, outer)
        sum_scores()
        if planes > 1:
            z_sent()
        for kind, first, count in ((0, 0, pushed), (1, pushed, quarters - pushed)):
            lanes = pl.ds(first * part_lanes, count * part_lanes)
            if count:
                await_sent(picked.at[0, :, lanes], psent.at[0, kind], True if kind else no(outer))
                for n in (1, 2):
                    if not kind:
                        await_sent(picked.at[n, :, lanes], psent.at[n, kind], inner)
        for condition, copy in sent:
            when(condition, copy.wait_send)
        for condition, copy in head_copies():
            when(condition, copy.wait_send)
        pltpu.make_async_copy(found, out, wsent.at[0]).wait()

    share_scores()
    drain()


def body(
    activations,
    out_grads,
    proj_in,
    proj_out,
    left_factor,
    right_factor,
    seq_lengths,
    seq_slots,
    stored_grads,
):
    dma = pltpu.SemaphoreType.DMA
    feats, toks = lax.axis_size("feat"), lax.axis_size("tok")
    rank = right_factor.shape[0]
    tok_rows = activations.shape[0]
    seqs = seq_lengths.shape[0]
    local = seqs // toks
    chunk = tok_rows // local
    store_rows, width = stored_grads.shape
    planes, chips = toks // 2, feats // 2
    wide = rank // feats
    quarters = wide // 16
    tiles = rank // 128
    score_rows = store_rows // feats
    lanes = seqs + -seqs % 128
    half = chunk // 2
    steps = max(planes - 1, 1)
    pieces = width // 2 // (2 * rank)
    pushed = pushed_quarters(planes, quarters)
    aside = max(pushed, 1)
    aside_lanes = aside * 8 * rank

    def vmem(*shape, dtype=F32):
        return pltpu.VMEM(shape, dtype)

    scores, own_rows = pl.pallas_call(
        functools.partial(kernel, (toks, feats, local, chunk, rank, seqs, store_rows)),
        out_shape=[
            jax.ShapeDtypeStruct((score_rows, seqs), F32),
            jax.ShapeDtypeStruct((local, width), F32),
        ],
        in_specs=[ANY] * 9,
        out_specs=[VMEM, ANY],
        scratch_shapes=[
            vmem(*out_grads.shape, dtype=BF16),
            vmem(*activations.shape, dtype=BF16),
            vmem(*proj_out.shape, dtype=BF16),
            vmem(*proj_in.shape, dtype=BF16),
            vmem(rank, rank),
            vmem(rank, rank),
            vmem(1, seqs, dtype=jnp.int32),
            vmem(1, seqs, dtype=jnp.int32),
            vmem(2, rank, rank, dtype=BF16),
            vmem(3 * rank, rank, dtype=BF16),
            vmem(2, *proj_out.shape, dtype=BF16),
            vmem(local, 2, chips, wide, chunk),
            vmem(local, chips, wide, chunk),
            vmem(local, chips, wide, chunk),
            vmem(local, chips - 1, wide, chunk),
            vmem(local, wide, chunk),
            vmem(local, 2, half, rank),
            vmem(local, half, rank),
            vmem(local, half, rank),
            vmem(local, chips - 1, half, rank),
            vmem(local, 2, half, rank),
            vmem(local + 1, 2, quarters, tiles, 8, 128),
            vmem(quarters, tiles, 8, 128),
            vmem(quarters, tiles, 8, 128),
            vmem(quarters, tiles, seqs * 8, 128),
            vmem(store_rows, width // 2),
            vmem(store_rows, width // 2),
            vmem(2, store_rows, aside_lanes),
            vmem(4 * store_rows, width // 2, dtype=BF16),
            vmem(4 * store_rows, aside_lanes, dtype=BF16),
            vmem(planes, 4 * local, 4 * store_rows),
            vmem(planes, 4 * local, 4 * store_rows),
            vmem(local, width),
            vmem(3, local, width // 2),
            vmem(2, 2, feats, score_rows, lanes),
            vmem(2, 2 * feats, score_rows, lanes),
            dma((2 * (local // 2 if local % 2 == 0 else local) + 7,)),
            dma((2, local)),
            dma((2, local, chips - 1)),
            dma((local,)),
            dma((local,)),
            dma((2,)),
            dma((2, 2, local // 2 + 1)),
            dma((2, max(steps - 2, 1), quarters)),
            dma((4,)),
            dma((3, quarters)),
            dma((2,)),
            dma((2,)),
            dma((2, chips - 1)),
            dma((1,)),
            dma((1,)),
            dma((3,)),
            dma((2, 2, steps)),
            dma((4,)),
            dma((3, 2)),
            dma((2,)),
            dma((1,)),
        ],
        compiler_params=pltpu.CompilerParams(
            collective_id=0, has_side_effects=True, vmem_limit_bytes=60 << 20
        ),
        name="influence",
    )(
        out_grads, activations, proj_out, proj_in, left_factor, right_factor,
        seq_lengths.reshape(1, seqs), seq_slots.reshape(1, seqs), stored_grads,
    )
    return scores, own_rows


def solution(mesh):
    placed = (
        P("tok", "feat"),
        P("tok", "feat"),
        P("feat", None),
        P("feat", None),
        P(),
        P(),
        P(),
        P(),
        P("tok", "feat"),
    )
    return jax.shard_map(
        body,
        mesh=mesh,
        in_specs=placed,
        out_specs=(P(("tok", "feat"), None), P("tok", "feat")),
        check_vma=False,
    )
```

```python
import functools

import jax
import jax.numpy as jnp
from jax import lax
from jax.experimental import pallas as pl
from jax.experimental.pallas import tpu as pltpu
from jax.sharding import PartitionSpec as P

MESH = pl.DeviceIdType.MESH
VMEM = pl.BlockSpec(memory_space=pltpu.VMEM)
ANY = pl.BlockSpec(memory_space=pl.ANY)
F32, BF16 = jnp.float32, jnp.bfloat16
DOWN, UP = 0, 1


def halves(value):
    high = value.astype(BF16)
    return high, (value - high.astype(F32)).astype(BF16)


def times(left, right):
    return jnp.dot(left, right, preferred_element_type=F32)


def times_t(left, right):
    return lax.dot_general(left, right, (((1,), (1,)), ((), ())), preferred_element_type=F32)


def stack_left(value, axis):
    high, low = halves(value)
    return jnp.concatenate([high, low, high], axis=axis)


def stack_right(value, axis):
    high, low = halves(value)
    return jnp.concatenate([high, high, low], axis=axis)


def aligned(index, size):
    return pl.ds(pl.multiple_of(index * size, size), size)


def pushed_quarters(planes, quarters):
    return quarters // 2 if planes == 4 else 0


def both(first, second):
    if first is True:
        return second
    if second is True:
        return first
    return False if first is False or second is False else first & second


def no(value):
    return not value if isinstance(value, bool) else jnp.logical_not(value)


def when(condition, action):
    if condition is True:
        action()
    elif condition is not False:
        pl.when(condition)(action)


def kernel(dims, *refs):
    toks, feats, local, chunk, rank, seqs, store_rows = dims
    out_rows, in_rows, out_mat, in_mat, left_hbm, right_hbm, lens_hbm, slots_hbm, stored = refs[:9]
    total, out = refs[9:11]
    lhs_o, lhs_i, rhs_o, rhs_i, left_f, right_f, lens, slots = refs[11:19]
    left_cat, right_cat, folded = refs[19:22]
    lp, la, ly, lb, lfin = refs[22:27]
    rp, ra, ry, rb, rfull = refs[27:32]
    block, hx, hz, gs = refs[32:36]
    kept, given, guest, mats, guest_mats, sc, guest_sc = refs[36:43]
    picked, scored, landed = refs[43:46]
    load, asem, bsem, csem, xsem, hsem, zrecv, zlast, srecv, precv, rrecv = refs[46:57]
    asent, bsent, csent, xsent, hsent, zsent, ssent, psent, rsent = refs[57:]

    tok, feat = lax.axis_index("tok"), lax.axis_index("feat")
    plane, x = tok // 2, tok % 2
    y, c = feat // 2, feat % 2
    planes = toks // 2
    mate, chips = feat + 1 - 2 * c, feats // 2
    across = [(y + turn) % chips for turn in range(1, chips)]
    beside = tok + 1 - 2 * x
    wide = rank // feats
    half_o = wide // 2
    quarters = half_o // 8
    in_plane = 2 * local
    half_lanes = half_o * rank
    part_lanes = 8 * rank
    tiles = rank // 128
    below, above = plane > 0, plane < planes - 1
    pushed = pushed_quarters(planes, quarters)
    outer = inner = False
    if pushed:
        outer = (plane == 0) | (plane == planes - 1)
        inner = (plane == 1) | (plane == planes - 2)
    partner = jnp.where(plane == 0, 1, jnp.where(
        plane == planes - 1, planes - 2, jnp.where(plane == 1, 0, planes - 1)))

    def remote(src, dst, sems, to_tok, to_feat):
        return pltpu.make_async_remote_copy(
            src_ref=src, dst_ref=dst, send_sem=sems[0], recv_sem=sems[1],
            device_id=(to_tok, to_feat), device_id_type=MESH,
        )

    loads = {}
    span = 2 if local % 2 == 0 else 1
    blocks = local // span
    tall = span * chunk

    def fetch(key, src, dst):
        loads[key] = pltpu.make_async_copy(src, dst, load.at[len(loads)])
        loads[key].start()

    def fetch_block(b):
        if b < blocks:
            rows = pl.ds(b * tall, tall)
            if b:
                fetch(("o", b), out_rows.at[rows], lhs_o.at[rows])
            fetch(("i", b), in_rows.at[rows], lhs_i.at[rows])

    fetch("left", left_hbm, left_f)
    fetch("out", out_mat, rhs_o)
    fetch(("o", 0), out_rows.at[pl.ds(0, tall)], lhs_o.at[pl.ds(0, tall)])
    fetch("in", in_mat, rhs_i)
    fetch_block(0)
    fetch("lens", lens_hbm, lens)
    fetch("slots", slots_hbm, slots)
    fetch("right", right_hbm, right_f)

    barrier = pltpu.get_barrier_semaphore()

    def greet(to_tok, to_feat):
        pl.semaphore_signal(barrier, inc=1, device_id=(to_tok, to_feat), device_id_type=MESH)

    for step in range(2):
        for turn in range(feats):
            if step or turn:
                greet(beside if step else tok, (feat + turn) % feats)
    met = 2 * feats - 1
    for side, there, crossing in ((-1, below, 0), (1, above, 1)):
        near = False
        if pushed:
            near = (outer & (partner == plane + side)) | (inner & (partner == plane + side))
        plain = both(there, no(near))
        corner = both(plain, x == crossing)
        met += plain.astype(jnp.int32) + corner.astype(jnp.int32)

        def greet_all(side=side):
            for other in range(2):
                for f in range(feats):
                    greet((plane + side) * 2 + other, f)

        if pushed:
            met += 2 * feats * near.astype(jnp.int32)
        when(near, greet_all)
        when(plain, lambda side=side: greet(tok + 2 * side, feat))
        when(corner, lambda side=side: greet(tok + side, feat))

    sent = []

    def start(copy, condition=True):
        when(condition, copy.start)
        return copy

    def await_sent(src, sem, condition=True):
        copy = remote(src, src, (sem, sem), tok, mate)
        sent.append((condition, copy))

    def await_all(dst, sem, condition=True):
        copy = remote(dst, dst, (sem, sem), tok, mate)
        when(condition, copy.wait_recv)

    piece = 2 * rank
    pieces = half_lanes // piece
    aside = pushed * part_lanes // piece
    trades = []

    def column(half, first, count=1):
        lanes = half * half_lanes + first * piece
        return pl.ds(pl.multiple_of(lanes, piece), piece * count)

    def push_own():
        copy = remote(
            stored.at[:, column(x, 0, aside)], guest.at[0], (ssent.at[2], srecv.at[2]),
            partner * 2 + x, feat)
        start(copy, outer)
        await_sent(stored.at[:, column(x, 0, aside)], ssent.at[2], outer)

    batches = 4 if pushed else 0
    batch = aside // 4

    def batch_lanes(n):
        return pl.ds(n * batch * piece, batch * piece)

    def push_given(n):
        lanes = batch_lanes(n)
        await_all(given.at[:, lanes], srecv.at[4 + n], outer)
        start(remote(
            given.at[:, lanes], guest.at[1, :, lanes], (ssent.at[3], srecv.at[3]),
            partner * 2 + x, feat), outer)

    def trade(count):
        for _ in range(count):
            n = len(trades)
            if n < pieces:
                kind = 0 if n < aside else 1
                trades.append(start(remote(
                    stored.at[:, column(1 - x, n)], given.at[:, pl.ds(n * piece, piece)],
                    (ssent.at[kind], srecv.at[1 if kind else 4 + n // batch]), beside, feat,
                )))

    def trades_sent():
        if aside:
            await_sent(stored.at[:, column(1 - x, 0, aside)], ssent.at[0])
            await_sent(given.at[:, pl.ds(0, aside * piece)], ssent.at[3], outer)
        await_sent(stored.at[:, column(1 - x, aside, pieces - aside)], ssent.at[1])

    copies = {}

    def fold_left():
        loads["left"].wait()
        for core in range(2):
            for side in range(chips):
                rows = left_f[pl.ds((side * 2 + core) * wide, wide), :]
                high, low = halves(rows)
                left_cat[0, pl.ds((core * chips + side) * wide, wide), :] = high
                left_cat[1, pl.ds((core * chips + side) * wide, wide), :] = low
        loads["out"].wait()
        depth = rhs_o.shape[0]
        step = min(256, depth)
        for n in range(depth // step):
            rows = rhs_o[pl.ds(n * step, step), :]
            folded[0, pl.ds(n * step, step), :], folded[1, pl.ds(n * step, step), :] = halves(
                times_t(rows, left_cat[0]) + times_t(rows, left_cat[1]))

    def project_out(b):
        loads["o", b].wait()
        own = [lhs_o[pl.ds((b * span + n) * chunk, chunk), :] for n in range(span)]
        sums = [times(rows, folded[0]) + times(rows, folded[1]) for rows in own]
        for n in range(span):
            lp[b * span + n] = jnp.transpose(sums[n]).reshape(2, chips, wide, chunk)

    def send_left(b):
        for k in range(b * span, b * span + span):
            copies["a", 0, k] = start(remote(
                lp.at[k, 1 - c], la.at[k], (asent.at[0], asem.at[0, k]), tok, mate))

    def pair_left(k):
        copies["a", 0, k].wait_recv()
        ly[k] = lp[k, c] + la[k]
        for n, other in enumerate(across):
            copies["b", 0, k, n] = start(remote(
                ly.at[k, other], lb.at[k, n], (bsent.at[0, n], bsem.at[0, k, n]),
                tok, other * 2 + c))

    def project_in(b):
        if b == 0:
            loads["in"].wait()
        loads["i", b].wait()
        if b == 0:
            fetch_block(1)
        fetch_block(b + 2)
        own = [lhs_i[pl.ds((b * span + n) * chunk, chunk), :] for n in range(span)]
        for n, sums in enumerate([times(rows, rhs_i[...]) for rows in own]):
            rp[b * span + n] = sums.reshape(2, chunk // 2, rank)

    def send_right(b):
        for k in range(b * span, b * span + span):
            copies["a", 1, k] = start(remote(
                rp.at[k, 1 - c], ra.at[k], (asent.at[1], asem.at[1, k]), tok, mate))

    def pair_right(k):
        copies["a", 1, k].wait_recv()
        ry[k] = rp[k, c] + ra[k]
        for n, other in enumerate(across):
            copies["b", 1, k, n] = start(remote(
                ry.at[k], rb.at[k, n], (bsent.at[1, n], bsem.at[1, k, n]),
                tok, other * 2 + c))

    def rows_sent():
        for side, ref in ((0, lp), (1, rp)):
            await_sent(ref.at[:, 1 - c], asent.at[side])
        for n, other in enumerate(across):
            await_sent(ly.at[:, other], bsent.at[0, n])
            await_sent(ry, bsent.at[1, n])
        await_sent(rfull.at[:, c], csent.at[0])
        await_sent(block.at[pl.ds(0, local), 1 - x], xsent.at[0])

    def finish_rows(k):
        if k == 0:
            loads["right"].wait()
            right_cat[...] = stack_right(right_f[...], 0)
        left, rows = ly[k, y], ry[k]
        for n in range(chips - 1):
            copies["b", 0, k, n].wait_recv()
            left += lb[k, n]
        lfin[k] = left
        for n in range(chips - 1):
            copies["b", 1, k, n].wait_recv()
            rows += rb[k, n]
        rfull[k, c] = times(stack_left(rows, 1), right_cat[...])
        copies["c", k] = start(remote(
            rfull.at[k, c], rfull.at[k, c], (csent.at[0], csem.at[k]), tok, mate))

    spans = {}

    def starts_of():
        loads["lens"].wait()
        lengths = lens[...].astype(F32)
        number = lax.broadcasted_iota(jnp.int32, (local, seqs), 1)
        mine = lax.broadcasted_iota(jnp.int32, (local, seqs), 0) + tok * local

        def pick(mask):
            return jnp.sum(jnp.where(mask, lengths, 0.0), axis=1, keepdims=True)

        spans["start"] = pick(number < mine)
        spans["now"] = 1.0 / jnp.maximum(pick(number == mine), 1.0)
        spans["before"] = 1.0 / jnp.maximum(pick(number == mine - 1), 1.0)

    def seq_rows(at_plane, number, side, count=1):
        first = (at_plane * in_plane + number * 2 + side) * 8
        return pl.ds(pl.multiple_of(first, 8), 8 * count)

    def settle(k, value):
        for tile in range(tiles):
            part = value[:, tile * 128 : (tile + 1) * 128]
            block[k, :, :, tile] = part.reshape(2, quarters, 8, 128)
        if k < local:
            gs[:, :, seq_rows(plane, k, x), :] = block[k, x]
            copies["x", k] = start(remote(
                block.at[k, 1 - x], gs.at[:, :, seq_rows(plane, k, x), :],
                (xsent.at[0], xsem.at[k]), beside, feat))

    def head_copies():
        return (
            (x == 1, remote(block.at[local, 0], hx, (hsent.at[0], hsem.at[0]), beside, feat)),
            ((x == 0) & below, remote(
                block.at[local, 0], hz, (hsent.at[1], hsem.at[1]), tok - 2, feat)),
            ((x == 0) & below, remote(
                block.at[local, 1], hz, (hsent.at[2], hsem.at[1]), tok - 1, feat)),
        )

    carry = {}

    def gradients(k):
        if k == 0:
            starts_of()
        copies["c", k].wait_recv()
        places = lax.broadcasted_iota(jnp.int32, (1, chunk), 1) + (tok * local + k) * chunk
        inside = places.astype(F32) >= spans["start"][k : k + 1]
        now = jnp.where(inside, spans["now"][k : k + 1], 0.0)
        before = jnp.where(inside, 0.0, spans["before"][k : k + 1])
        left = lfin[k]
        weighted = jnp.concatenate([left * now, left * before], axis=0)
        right = rfull[k].reshape(chunk, rank)
        both = times(stack_left(weighted, 1), stack_right(right, 0))
        tail = both[wide:]
        if k:
            settle(k - 1, carry["sum"] + tail)
        else:
            settle(local, tail)
            for condition, copy in head_copies():
                when(condition, copy.start)
        carry["sum"] = both[:wide]
        if k == local - 1:
            settle(k, carry["sum"])

    ways = (DOWN, UP)

    def block_plane(way, step):
        return jnp.clip(plane + step if way == DOWN else plane - step, 0, planes - 1)

    def to_outer(way):
        return (plane == 1 if way == DOWN else plane == planes - 2) if pushed else False

    def sending(way, step, kind=1):
        if way == DOWN:
            base = below & (plane + step < planes)
        else:
            base = above & (plane - step >= 0)
        return base if kind else both(base, no(to_outer(way)))

    def taking(way, step, kind=1):
        base = plane + 1 + step < planes if way == DOWN else plane - 1 - step >= 0
        return base if kind else both(base, no(outer))

    groups = local // 2
    tail_parts = range(pushed, quarters)
    kinds = (0, 1) if pushed else (1,)

    def z_data(at, kind, first, count):
        which = pl.ds(pushed, quarters - pushed) if kind else pl.ds(0, pushed)
        return gs.at[which, :, seq_rows(at, first, 0, 2 * count), :]

    def z_start(way, step, kind, first, count, part=None):
        data = z_data(block_plane(way, step), kind, first, count)
        came = zrecv.at[way, kind, step, first // 2]
        if part is not None:
            data = gs.at[part, :, seq_rows(block_plane(way, step), first, 0, 2 * count), :]
            came = zlast.at[way, part]
        copy = remote(
            data, data, (zsent.at[way, kind, step], came),
            tok - 2 if way == DOWN else tok + 2, feat)
        when(sending(way, step, kind), copy.start)

    def z_sent():
        for step in range(last_step + 1):
            for way in ways:
                for kind in kinds:
                    if kind or step < 2:
                        data = z_data(block_plane(way, step), kind, 0, local)
                        await_sent(data, zsent.at[way, kind, step], sending(way, step, kind))

    last_step = max(planes - 2, 0)

    def complete(k):
        copies["x", k].wait_recv()
        if k == local - 1:
            @pl.when(x == 1)
            def _():
                gs[:, :, seq_rows(plane, k, 0), :] += block[local, 1]

            @pl.when(x == 0)
            def _():
                head_copies()[0][1].wait_recv()
                gs[:, :, seq_rows(plane, k, 0), :] += hx[...]

            @pl.when(above)
            def _():
                head_copies()[1][1].wait_recv()
                gs[:, :, seq_rows(plane, k, 1), :] += hz[...]
        if planes > 1:
            for kind in kinds:
                for way in ways:
                    z_start(way, 0, kind, k, 1)

    def take(step, kind, group):
        for way in ways:
            data = z_data(block_plane(way, step + 1), kind, 2 * group, 2)
            await_all(data, zrecv.at[way, kind, step, group], taking(way, step, kind))

    whole_groups = groups - 1 if last_step >= 2 else groups

    def pass_on(step, group, only=kinds):
        if planes > 1 and step <= last_step:
            for kind in only:
                if kind or step < 2:
                    take(step, kind, group)
                if step < last_step and (kind or step + 1 < 2):
                    split = step + 1 == last_step and last_step >= 2
                    for way in ways:
                        if not split or group < whole_groups:
                            z_start(way, step + 1, kind, 2 * group, 2)
                    if split and group == groups - 1:
                        for part in tail_parts:
                            for way in ways:
                                z_start(way, step + 1, kind, 2 * whole_groups,
                                        local - 2 * whole_groups, part)

    def take_last(part):
        first = 2 * whole_groups
        for way in ways:
            at = block_plane(way, last_step + 1)
            data = gs.at[part, :, seq_rows(at, first, 0, 2 * (local - first)), :]
            await_all(data, zlast.at[way, part], taking(way, last_step))

    def make_mats(target, rows, lanes, value):
        high, low = halves(value)
        count = 2 * store_rows
        target[pl.ds(rows * store_rows, store_rows), lanes] = high
        target[pl.ds(count + rows * store_rows, store_rows), lanes] = low

    def score(target, at, part):
        lines = []
        for line in range(8):
            first = at * in_plane * 8 + line
            for tile in range(tiles):
                lines.append(gs[part, tile, pl.ds(first, in_plane, stride=8), :])
        high, low = halves(jnp.concatenate(lines, axis=1))
        return times_t(
            jnp.concatenate([high, low], axis=0),
            target[:, pl.ds(part * part_lanes, part_lanes)],
        )

    def score_plane(at):
        value = score(mats, at, pushed)
        for part in range(pushed + 1, quarters):
            value += score(mats, at, part)
        sc[at] = value

        def more():
            value = score(mats, at, 0)
            for part in range(1, pushed):
                value += score(mats, at, part)
            sc[at] += value

        if pushed:
            when(no(outer), more)

    def score_guests():
        for step in range(2):
            await_all(guest.at[step], srecv.at[2 + step])
        lanes = pl.ds(0, pushed * part_lanes)
        for step in range(2):
            make_mats(guest_mats, step, lanes, guest[step])
        for at in range(planes):
            value = score(guest_mats, at, 0)
            for part in range(1, pushed):
                value += score(guest_mats, at, part)
            guest_sc[at] = value

    def score_step(step):
        for way in ways:
            when(taking(way, step), lambda way=way: score_plane(block_plane(way, step + 1)))

    def stage_rows(k):
        if 0 <= k < local:
            finish_rows(k)

    def stage_grads(k):
        if 0 <= k < local:
            gradients(k)
            if k % 2 and 1 < k < local - 2:
                trade(1)

    def stage_complete(k):
        if 0 <= k < local:
            complete(k)

    fold_left()
    project_out(0)
    pl.semaphore_wait(barrier, met)
    send_left(0)
    if pushed:
        push_own()
    trade(3)
    early = min(2, local) if blocks >= 3 else 0
    for b in range(blocks):
        chunks = range(b * span, b * span + span)
        if b == 0:
            for k in chunks:
                pair_left(k)
        project_in(b)
        send_right(b)
        if b:
            for k in chunks:
                pair_left(k)
        if b == 1:
            trade(2)
        if b == blocks - 2 and early:
            stage_rows(0)
        if b + 1 < blocks:
            project_out(b + 1)
            send_left(b + 1)
        else:
            fetch("kept", stored.at[:, column(x, 0, pieces)], kept)
        for k in chunks:
            pair_right(k)
        if b == blocks - 2 and early:
            stage_grads(0)
            stage_rows(1)
    if early:
        stage_grads(1)
    passed = 0
    for k in range(early, local):
        stage_complete(k - 3)
        stage_rows(k)
        stage_grads(k)
        if k >= 5 and k % 2:
            pass_on(0, (k - 5) // 2)
            passed = (k - 5) // 2 + 1
    trade(pieces)
    trades_sent()
    rows_sent()
    stage_complete(local - 3)
    loads["kept"].wait()
    make_mats(mats, 0, pl.ds(0, half_lanes), kept[...])
    for group in range(passed, groups - 2):
        pass_on(0, group)
    passed = max(passed, groups - 2)
    stage_complete(local - 2)
    stage_complete(local - 1)
    for n in range(batches):
        push_given(n)
    pass_on(1, 0, (1,))

    loads["slots"].wait()
    at_row = lax.broadcasted_iota(jnp.int32, (seqs, seqs), 1)
    seq_of = ((at_row // in_plane) * 2 + at_row % 2) * local + (at_row % in_plane) // 2
    by_seq = jnp.where(lax.broadcasted_iota(jnp.int32, (seqs, seqs), 0) == seq_of, 1.0, 0.0)
    by_seq = by_seq.astype(BF16)
    slot = lax.broadcasted_iota(jnp.int32, (seqs, seqs), 0)
    by_slot = times(
        jnp.where(slots[...] == slot, 1.0, 0.0).astype(BF16), by_seq)
    row = lax.broadcasted_iota(jnp.int32, (4 * local, seqs), 0)
    wanted = jnp.zeros((4 * local, seqs), jnp.int32)
    for n, owner in enumerate((tok, beside, partner * 2 + x, partner * 2 + 1 - x)):
        here = (row >= n * local) & (row < (n + 1) * local)
        wanted = jnp.where(here, owner * local + row - n * local, wanted)
    pick = times(
        jnp.where(slots[...] == wanted, 1.0, 0.0).astype(BF16), by_seq).astype(BF16)
    pick = jnp.concatenate([pick, pick], axis=1)

    for group in range(passed, groups):
        pass_on(0, group)
        pass_on(1, group - 1, (1,))

    def given_mats(first, count):
        lanes = pl.ds(first * part_lanes, count * part_lanes)
        make_mats(mats, 1, lanes, given[:, lanes])

    def give(part, n, to, condition):
        lane = part * part_lanes
        there = pl.ds(pl.multiple_of(x * half_lanes + lane, part_lanes), part_lanes)
        sem = psent.at[n, 0 if part < pushed else 1]
        copies["p", n, part] = start(remote(
            picked.at[n, :, pl.ds(lane, part_lanes)], out.at[:, there],
            (sem, precv.at[n, part]), to, feat), condition)

    def fill_rows(part):
        count = 4 if part < pushed else 2
        for line in range(8):
            high, low = halves(jnp.concatenate(
                [gs[part, tile, pl.ds(line, seqs, stride=8), :] for tile in range(tiles)], axis=1))
            taken = times(pick[: count * local], jnp.concatenate([high, low], axis=0))
            lane = part * part_lanes + line * rank
            out[:, pl.ds(pl.multiple_of(x * half_lanes + lane, rank), rank)] = taken[:local]
            for n in range(1, count):
                picked[n - 1, :, pl.ds(lane, rank)] = taken[n * local : (n + 1) * local]

    def hand_rows(part, condition):
        if part < pushed:
            give(part, 1, partner * 2 + x, inner)
            give(part, 2, partner * 2 + 1 - x, inner)
        give(part, 0, beside, condition)

    def rows_for_slots(part):
        condition = no(outer) if part < pushed else True
        when(condition, lambda: fill_rows(part))
        hand_rows(part, condition)

    def turn_scores(sums):
        count = 2 * store_rows
        high, low = sums[:, :in_plane], sums[:, in_plane:]
        by_row = (high[:, :, :count] + high[:, :, count:] + low[:, :, :count]).reshape(seqs, count)
        lanes = scored.shape[4]
        placed = jnp.dot(
            by_slot, by_row, precision=lax.Precision.HIGHEST, preferred_element_type=F32)
        if lanes > seqs:
            placed = jnp.concatenate([placed, jnp.zeros((lanes - seqs, count), F32)], axis=0)
        return jnp.transpose(
            jnp.concatenate([placed, jnp.zeros((lanes, 128 - count), F32)], axis=1))

    few = scored.shape[3]
    parts = {}

    def send_scores(kind, own, condition):
        base = partner if kind else plane
        for step in range(2):
            for turn in range(feats):
                if kind or step or turn:
                    to = (feat + turn) % feats
                    parts[kind, step, turn] = start(remote(
                        scored.at[kind, step, to], landed.at[kind, step * feats + turn],
                        (rsent.at[kind], rrecv.at[kind]),
                        base * 2 + (1 - x if step else x), to,
                    ), condition)
        first = 0 if kind else 1
        await_sent(landed.at[kind, pl.ds(first, 2 * feats - first)], rsent.at[kind], condition)

    def place_scores(kind, sums):
        turned = turn_scores(sums)
        for step in range(2):
            for f in range(feats):
                first = (step * feats + f) * few
                scored[kind, step, f] = turned[first : first + few]

    def share_guests():
        when(inner, lambda: place_scores(1, guest_sc[...]))
        send_scores(1, guest_sc, inner)

    def share_scores():
        place_scores(0, sc[...])
        send_scores(0, sc, True)

    if pushed:
        for group in range(groups):
            pass_on(1, group, (0,))
        for part in range(pushed):
            rows_for_slots(part)
        pass_on(1, groups - 1, (1,))
        when(inner, score_guests)
        share_guests()
        when(inner, lambda: [fill_rows(part) for part in tail_parts] and None)
        for part in tail_parts:
            hand_rows(part, inner)
    else:
        pass_on(1, groups - 1, (1,))
    for n in range(batches):
        await_all(given.at[:, batch_lanes(n)], srecv.at[4 + n], no(outer))
    await_all(given.at[:, pl.ds(aside * piece, (pieces - aside) * piece)], srecv.at[1])
    given_mats(pushed, quarters - pushed)
    if pushed:
        when(no(outer), lambda: given_mats(0, pushed))
    score_plane(plane)
    score_step(0)
    if last_step > 0:
        score_step(1)
    for step in range(2, last_step + 1):
        for group in range(groups if step < last_step else whole_groups):
            pass_on(step, group)
        if step < last_step:
            score_step(step)
    for part in tail_parts:
        if last_step >= 2:
            take_last(part)
        if pushed:
            when(outer, lambda part=part: fill_rows(part))
            hand_rows(part, outer)
        else:
            rows_for_slots(part)
    if last_step >= 2:
        score_step(last_step)

    def sum_scores():
        others = pl.ds(1, 2 * feats - 1)
        await_all(landed.at[0, others], rrecv.at[0])
        summed = scored[0, 0, feat]
        for n in range(1, 2 * feats):
            summed += landed[0, n]
        total[...] = summed[:, :seqs]

        def add_more():
            await_all(landed.at[1], rrecv.at[1])
            more = landed[1, 0]
            for n in range(1, 2 * feats):
                more += landed[1, n]
            total[...] += more[:, :seqs]

        if pushed:
            when(outer, add_more)

    def drain():
        for part in range(quarters):
            arrives = no(outer) if part < pushed else True
            when(arrives, copies["p", 0, part].wait_recv)
        for part in range(pushed):
            for n in (1, 2):
                when(outer, copies["p", n, part].wait_recv)
        sum_scores()
        if planes > 1:
            z_sent()
        for kind, first, count in ((0, 0, pushed), (1, pushed, quarters - pushed)):
            lanes = pl.ds(first * part_lanes, count * part_lanes)
            if count:
                await_sent(picked.at[0, :, lanes], psent.at[0, kind], True if kind else no(outer))
                for n in (1, 2):
                    if not kind:
                        await_sent(picked.at[n, :, lanes], psent.at[n, kind], inner)
        for condition, copy in sent:
            when(condition, copy.wait_send)
        for condition, copy in head_copies():
            when(condition, copy.wait_send)

    share_scores()
    drain()


def body(
    activations,
    out_grads,
    proj_in,
    proj_out,
    left_factor,
    right_factor,
    seq_lengths,
    seq_slots,
    stored_grads,
):
    dma = pltpu.SemaphoreType.DMA
    feats, toks = lax.axis_size("feat"), lax.axis_size("tok")
    rank = right_factor.shape[0]
    tok_rows = activations.shape[0]
    seqs = seq_lengths.shape[0]
    local = seqs // toks
    chunk = tok_rows // local
    store_rows, width = stored_grads.shape
    planes, chips = toks // 2, feats // 2
    wide = rank // feats
    quarters = wide // 16
    tiles = rank // 128
    score_rows = store_rows // feats
    lanes = seqs + -seqs % 128
    half = chunk // 2
    steps = max(planes - 1, 1)
    pieces = width // 2 // (2 * rank)
    pushed = pushed_quarters(planes, quarters)
    aside = max(pushed, 1)
    aside_lanes = aside * 8 * rank

    def vmem(*shape, dtype=F32):
        return pltpu.VMEM(shape, dtype)

    scores, own_rows = pl.pallas_call(
        functools.partial(kernel, (toks, feats, local, chunk, rank, seqs, store_rows)),
        out_shape=[
            pltpu.VMEM((score_rows, seqs), F32),
            pltpu.VMEM((local, width), F32),
        ],
        in_specs=[ANY] * 9,
        out_specs=[VMEM, VMEM],
        scratch_shapes=[
            vmem(*out_grads.shape, dtype=BF16),
            vmem(*activations.shape, dtype=BF16),
            vmem(*proj_out.shape, dtype=BF16),
            vmem(*proj_in.shape, dtype=BF16),
            vmem(rank, rank),
            vmem(rank, rank),
            vmem(1, seqs, dtype=jnp.int32),
            vmem(1, seqs, dtype=jnp.int32),
            vmem(2, rank, rank, dtype=BF16),
            vmem(3 * rank, rank, dtype=BF16),
            vmem(2, *proj_out.shape, dtype=BF16),
            vmem(local, 2, chips, wide, chunk),
            vmem(local, chips, wide, chunk),
            vmem(local, chips, wide, chunk),
            vmem(local, chips - 1, wide, chunk),
            vmem(local, wide, chunk),
            vmem(local, 2, half, rank),
            vmem(local, half, rank),
            vmem(local, half, rank),
            vmem(local, chips - 1, half, rank),
            vmem(local, 2, half, rank),
            vmem(local + 1, 2, quarters, tiles, 8, 128),
            vmem(quarters, tiles, 8, 128),
            vmem(quarters, tiles, 8, 128),
            vmem(quarters, tiles, seqs * 8, 128),
            vmem(store_rows, width // 2),
            vmem(store_rows, width // 2),
            vmem(2, store_rows, aside_lanes),
            vmem(4 * store_rows, width // 2, dtype=BF16),
            vmem(4 * store_rows, aside_lanes, dtype=BF16),
            vmem(planes, 4 * local, 4 * store_rows),
            vmem(planes, 4 * local, 4 * store_rows),
            vmem(3, local, width // 2),
            vmem(2, 2, feats, score_rows, lanes),
            vmem(2, 2 * feats, score_rows, lanes),
            dma((2 * (local // 2 if local % 2 == 0 else local) + 7,)),
            dma((2, local)),
            dma((2, local, chips - 1)),
            dma((local,)),
            dma((local,)),
            dma((2,)),
            dma((2, 2, steps, (local + 1) // 2)),
            dma((2, quarters)),
            dma((8,)),
            dma((3, quarters)),
            dma((2,)),
            dma((2,)),
            dma((2, chips - 1)),
            dma((1,)),
            dma((1,)),
            dma((3,)),
            dma((2, 2, steps)),
            dma((4,)),
            dma((3, 2)),
            dma((2,)),
        ],
        compiler_params=pltpu.CompilerParams(
            collective_id=0, has_side_effects=True, vmem_limit_bytes=60 << 20
        ),
        name="influence",
    )(
        out_grads, activations, proj_out, proj_in, left_factor, right_factor,
        seq_lengths.reshape(1, seqs), seq_slots.reshape(1, seqs), stored_grads,
    )
    return scores, own_rows


def solution(mesh):
    placed = (
        P("tok", "feat"),
        P("tok", "feat"),
        P("feat", None),
        P("feat", None),
        P(),
        P(),
        P(),
        P(),
        P("tok", "feat"),
    )
    return jax.shard_map(
        body,
        mesh=mesh,
        in_specs=placed,
        out_specs=(P(("tok", "feat"), None), P("tok", "feat")),
        check_vma=False,
    )
```

```python
import functools

import jax
import jax.numpy as jnp
from jax import lax
from jax.experimental import pallas as pl
from jax.experimental.pallas import tpu as pltpu
from jax.sharding import PartitionSpec as P

MESH = pl.DeviceIdType.MESH
VMEM = pl.BlockSpec(memory_space=pltpu.VMEM)
ANY = pl.BlockSpec(memory_space=pl.ANY)
F32, BF16 = jnp.float32, jnp.bfloat16
DOWN, UP = 0, 1


def halves(value):
    high = value.astype(BF16)
    return high, (value - high.astype(F32)).astype(BF16)


def times(left, right):
    return jnp.dot(left, right, preferred_element_type=F32)


def times_t(left, right):
    return lax.dot_general(left, right, (((1,), (1,)), ((), ())), preferred_element_type=F32)


def stack_left(value, axis):
    high, low = halves(value)
    return jnp.concatenate([high, low, high], axis=axis)


def stack_right(value, axis):
    high, low = halves(value)
    return jnp.concatenate([high, high, low], axis=axis)


def aligned(index, size):
    return pl.ds(pl.multiple_of(index * size, size), size)


def pushed_quarters(planes, quarters):
    return quarters // 2 if planes == 4 else 0


def both(first, second):
    if first is True:
        return second
    if second is True:
        return first
    return False if first is False or second is False else first & second


def no(value):
    return not value if isinstance(value, bool) else jnp.logical_not(value)


def when(condition, action):
    if condition is True:
        action()
    elif condition is not False:
        pl.when(condition)(action)


def kernel(dims, *refs):
    toks, feats, local, chunk, rank, seqs, store_rows = dims
    out_rows, in_rows, out_mat, in_mat, left_hbm, right_hbm, lens_hbm, slots_hbm, stored = refs[:9]
    total, out = refs[9:11]
    lhs_o, lhs_i, rhs_o, rhs_i, left_f, right_f, lens, slots = refs[11:19]
    left_cat, right_cat, folded = refs[19:22]
    lp, la, ly, lb, lfin = refs[22:27]
    rp, ra, ry, rb, rfull = refs[27:32]
    block, hx, hz, gs = refs[32:36]
    kept, given, guest, mats, guest_mats, sc, guest_sc = refs[36:43]
    picked, scored, landed = refs[43:46]
    load, asem, bsem, csem, xsem, hsem, zrecv, zlast, srecv, precv, rrecv = refs[46:57]
    asent, bsent, csent, xsent, hsent, zsent, ssent, psent, rsent = refs[57:]

    tok, feat = lax.axis_index("tok"), lax.axis_index("feat")
    plane, x = tok // 2, tok % 2
    y, c = feat // 2, feat % 2
    planes = toks // 2
    mate, chips = feat + 1 - 2 * c, feats // 2
    across = [(y + turn) % chips for turn in range(1, chips)]
    beside = tok + 1 - 2 * x
    wide = rank // feats
    half_o = wide // 2
    quarters = half_o // 8
    in_plane = 2 * local
    half_lanes = half_o * rank
    part_lanes = 8 * rank
    tiles = rank // 128
    below, above = plane > 0, plane < planes - 1
    pushed = pushed_quarters(planes, quarters)
    outer = inner = False
    if pushed:
        outer = (plane == 0) | (plane == planes - 1)
        inner = (plane == 1) | (plane == planes - 2)
    partner = jnp.where(plane == 0, 1, jnp.where(
        plane == planes - 1, planes - 2, jnp.where(plane == 1, 0, planes - 1)))

    def remote(src, dst, sems, to_tok, to_feat):
        return pltpu.make_async_remote_copy(
            src_ref=src, dst_ref=dst, send_sem=sems[0], recv_sem=sems[1],
            device_id=(to_tok, to_feat), device_id_type=MESH,
        )

    loads = {}
    span = 2 if local % 2 == 0 else 1
    blocks = local // span
    tall = span * chunk

    def fetch(key, src, dst):
        loads[key] = pltpu.make_async_copy(src, dst, load.at[len(loads)])
        loads[key].start()

    def fetch_block(b):
        if b < blocks:
            rows = pl.ds(b * tall, tall)
            if b:
                fetch(("o", b), out_rows.at[rows], lhs_o.at[rows])
            fetch(("i", b), in_rows.at[rows], lhs_i.at[rows])

    fetch("left", left_hbm, left_f)
    fetch("out", out_mat, rhs_o)
    fetch(("o", 0), out_rows.at[pl.ds(0, tall)], lhs_o.at[pl.ds(0, tall)])
    fetch("in", in_mat, rhs_i)
    fetch_block(0)
    fetch("lens", lens_hbm, lens)
    fetch("slots", slots_hbm, slots)
    fetch("right", right_hbm, right_f)

    barrier = pltpu.get_barrier_semaphore()

    def greet(to_tok, to_feat):
        pl.semaphore_signal(barrier, inc=1, device_id=(to_tok, to_feat), device_id_type=MESH)

    for step in range(2):
        for turn in range(feats):
            if step or turn:
                greet(beside if step else tok, (feat + turn) % feats)
    met = 2 * feats - 1
    for side, there, crossing in ((-1, below, 0), (1, above, 1)):
        near = False
        if pushed:
            near = (outer & (partner == plane + side)) | (inner & (partner == plane + side))
        plain = both(there, no(near))
        corner = both(plain, x == crossing)
        met += plain.astype(jnp.int32) + corner.astype(jnp.int32)

        def greet_all(side=side):
            for other in range(2):
                for f in range(feats):
                    greet((plane + side) * 2 + other, f)

        if pushed:
            met += 2 * feats * near.astype(jnp.int32)
        when(near, greet_all)
        when(plain, lambda side=side: greet(tok + 2 * side, feat))
        when(corner, lambda side=side: greet(tok + side, feat))

    sent = []

    def start(copy, condition=True):
        when(condition, copy.start)
        return copy

    def await_sent(src, sem, condition=True):
        copy = remote(src, src, (sem, sem), tok, mate)
        sent.append((condition, copy))

    def await_all(dst, sem, condition=True):
        copy = remote(dst, dst, (sem, sem), tok, mate)
        when(condition, copy.wait_recv)

    piece = 2 * rank
    pieces = half_lanes // piece
    aside = pushed * part_lanes // piece
    trades = []

    def column(half, first, count=1):
        lanes = half * half_lanes + first * piece
        return pl.ds(pl.multiple_of(lanes, piece), piece * count)

    def push_own():
        copy = remote(
            stored.at[:, column(x, 0, aside)], guest.at[0], (ssent.at[2], srecv.at[2]),
            partner * 2 + x, feat)
        start(copy, outer)
        await_sent(stored.at[:, column(x, 0, aside)], ssent.at[2], outer)

    batches = 4 if pushed else 0
    batch = aside // 4

    def batch_lanes(n):
        return pl.ds(n * batch * piece, batch * piece)

    def push_given(n):
        lanes = batch_lanes(n)
        await_all(given.at[:, lanes], srecv.at[4 + n], outer)
        start(remote(
            given.at[:, lanes], guest.at[1, :, lanes], (ssent.at[3], srecv.at[3]),
            partner * 2 + x, feat), outer)

    def trade(count):
        for _ in range(count):
            n = len(trades)
            if n < pieces:
                kind = 0 if n < aside else 1
                trades.append(start(remote(
                    stored.at[:, column(1 - x, n)], given.at[:, pl.ds(n * piece, piece)],
                    (ssent.at[kind], srecv.at[1 if kind else 4 + n // batch]), beside, feat,
                )))

    def trades_sent():
        if aside:
            await_sent(stored.at[:, column(1 - x, 0, aside)], ssent.at[0])
            await_sent(given.at[:, pl.ds(0, aside * piece)], ssent.at[3], outer)
        await_sent(stored.at[:, column(1 - x, aside, pieces - aside)], ssent.at[1])

    copies = {}

    def fold_left():
        loads["left"].wait()
        for core in range(2):
            for side in range(chips):
                rows = left_f[pl.ds((side * 2 + core) * wide, wide), :]
                high, low = halves(rows)
                left_cat[0, pl.ds((core * chips + side) * wide, wide), :] = high
                left_cat[1, pl.ds((core * chips + side) * wide, wide), :] = low
        loads["out"].wait()
        depth = rhs_o.shape[0]
        step = min(256, depth)
        for n in range(depth // step):
            rows = rhs_o[pl.ds(n * step, step), :]
            folded[0, pl.ds(n * step, step), :], folded[1, pl.ds(n * step, step), :] = halves(
                times_t(rows, left_cat[0]) + times_t(rows, left_cat[1]))

    def project_out(b):
        loads["o", b].wait()
        own = [lhs_o[pl.ds((b * span + n) * chunk, chunk), :] for n in range(span)]
        sums = [times(rows, folded[0]) + times(rows, folded[1]) for rows in own]
        for n in range(span):
            lp[b * span + n] = jnp.transpose(sums[n]).reshape(2, chips, wide, chunk)

    def send_left(b):
        for k in range(b * span, b * span + span):
            copies["a", 0, k] = start(remote(
                lp.at[k, 1 - c], la.at[k], (asent.at[0], asem.at[0, k]), tok, mate))

    def pair_left(k):
        copies["a", 0, k].wait_recv()
        ly[k] = lp[k, c] + la[k]
        for n, other in enumerate(across):
            copies["b", 0, k, n] = start(remote(
                ly.at[k, other], lb.at[k, n], (bsent.at[0, n], bsem.at[0, k, n]),
                tok, other * 2 + c))

    def project_in(b):
        if b == 0:
            loads["in"].wait()
        loads["i", b].wait()
        if b == 0:
            fetch_block(1)
        fetch_block(b + 2)
        own = [lhs_i[pl.ds((b * span + n) * chunk, chunk), :] for n in range(span)]
        for n, sums in enumerate([times(rows, rhs_i[...]) for rows in own]):
            rp[b * span + n] = sums.reshape(2, chunk // 2, rank)

    def send_right(b):
        for k in range(b * span, b * span + span):
            copies["a", 1, k] = start(remote(
                rp.at[k, 1 - c], ra.at[k], (asent.at[1], asem.at[1, k]), tok, mate))

    def pair_right(k):
        copies["a", 1, k].wait_recv()
        ry[k] = rp[k, c] + ra[k]
        for n, other in enumerate(across):
            copies["b", 1, k, n] = start(remote(
                ry.at[k], rb.at[k, n], (bsent.at[1, n], bsem.at[1, k, n]),
                tok, other * 2 + c))

    def rows_sent():
        for side, ref in ((0, lp), (1, rp)):
            await_sent(ref.at[:, 1 - c], asent.at[side])
        for n, other in enumerate(across):
            await_sent(ly.at[:, other], bsent.at[0, n])
            await_sent(ry, bsent.at[1, n])
        await_sent(rfull.at[:, c], csent.at[0])
        await_sent(block.at[pl.ds(0, local), 1 - x], xsent.at[0])

    def finish_rows(k):
        if k == 0:
            loads["right"].wait()
            right_cat[...] = stack_right(right_f[...], 0)
        left, rows = ly[k, y], ry[k]
        for n in range(chips - 1):
            copies["b", 0, k, n].wait_recv()
            left += lb[k, n]
        lfin[k] = left
        for n in range(chips - 1):
            copies["b", 1, k, n].wait_recv()
            rows += rb[k, n]
        rfull[k, c] = times(stack_left(rows, 1), right_cat[...])
        copies["c", k] = start(remote(
            rfull.at[k, c], rfull.at[k, c], (csent.at[0], csem.at[k]), tok, mate))

    spans = {}

    def starts_of():
        loads["lens"].wait()
        lengths = lens[...].astype(F32)
        number = lax.broadcasted_iota(jnp.int32, (local, seqs), 1)
        mine = lax.broadcasted_iota(jnp.int32, (local, seqs), 0) + tok * local

        def pick(mask):
            return jnp.sum(jnp.where(mask, lengths, 0.0), axis=1, keepdims=True)

        spans["start"] = pick(number < mine)
        spans["now"] = 1.0 / jnp.maximum(pick(number == mine), 1.0)
        spans["before"] = 1.0 / jnp.maximum(pick(number == mine - 1), 1.0)

    def seq_rows(at_plane, number, side, count=1):
        first = (at_plane * in_plane + number * 2 + side) * 8
        return pl.ds(pl.multiple_of(first, 8), 8 * count)

    def settle(k, value):
        for tile in range(tiles):
            part = value[:, tile * 128 : (tile + 1) * 128]
            block[k, :, :, tile] = part.reshape(2, quarters, 8, 128)
        if k < local:
            gs[:, :, seq_rows(plane, k, x), :] = block[k, x]
            copies["x", k] = start(remote(
                block.at[k, 1 - x], gs.at[:, :, seq_rows(plane, k, x), :],
                (xsent.at[0], xsem.at[k]), beside, feat))

    def head_copies():
        return (
            (x == 1, remote(block.at[local, 0], hx, (hsent.at[0], hsem.at[0]), beside, feat)),
            ((x == 0) & below, remote(
                block.at[local, 0], hz, (hsent.at[1], hsem.at[1]), tok - 2, feat)),
            ((x == 0) & below, remote(
                block.at[local, 1], hz, (hsent.at[2], hsem.at[1]), tok - 1, feat)),
        )

    carry = {}

    def gradients(k):
        if k == 0:
            starts_of()
        copies["c", k].wait_recv()
        places = lax.broadcasted_iota(jnp.int32, (1, chunk), 1) + (tok * local + k) * chunk
        inside = places.astype(F32) >= spans["start"][k : k + 1]
        now = jnp.where(inside, spans["now"][k : k + 1], 0.0)
        before = jnp.where(inside, 0.0, spans["before"][k : k + 1])
        left = lfin[k]
        weighted = jnp.concatenate([left * now, left * before], axis=0)
        right = rfull[k].reshape(chunk, rank)
        both = times(stack_left(weighted, 1), stack_right(right, 0))
        tail = both[wide:]
        if k:
            settle(k - 1, carry["sum"] + tail)
        else:
            settle(local, tail)
            for condition, copy in head_copies():
                when(condition, copy.start)
        carry["sum"] = both[:wide]
        if k == local - 1:
            settle(k, carry["sum"])

    ways = (DOWN, UP)

    def block_plane(way, step):
        return jnp.clip(plane + step if way == DOWN else plane - step, 0, planes - 1)

    def to_outer(way):
        return (plane == 1 if way == DOWN else plane == planes - 2) if pushed else False

    def sending(way, step, kind=1):
        if way == DOWN:
            base = below & (plane + step < planes)
        else:
            base = above & (plane - step >= 0)
        return base if kind else both(base, no(to_outer(way)))

    def taking(way, step, kind=1):
        base = plane + 1 + step < planes if way == DOWN else plane - 1 - step >= 0
        return base if kind else both(base, no(outer))

    groups = local // 2
    tail_parts = range(pushed, quarters)
    kinds = (0, 1) if pushed else (1,)

    def z_data(at, kind, first, count):
        which = pl.ds(pushed, quarters - pushed) if kind else pl.ds(0, pushed)
        return gs.at[which, :, seq_rows(at, first, 0, 2 * count), :]

    def z_start(way, step, kind, first, count, part=None):
        data = z_data(block_plane(way, step), kind, first, count)
        came = zrecv.at[way, kind, step, first // 2]
        if part is not None:
            data = gs.at[part, :, seq_rows(block_plane(way, step), first, 0, 2 * count), :]
            came = zlast.at[way, part]
        copy = remote(
            data, data, (zsent.at[way, kind, step], came),
            tok - 2 if way == DOWN else tok + 2, feat)
        when(sending(way, step, kind), copy.start)

    def z_sent():
        for step in range(last_step + 1):
            for way in ways:
                for kind in kinds:
                    if kind or step < 2:
                        data = z_data(block_plane(way, step), kind, 0, local)
                        await_sent(data, zsent.at[way, kind, step], sending(way, step, kind))

    last_step = max(planes - 2, 0)

    def complete(k):
        copies["x", k].wait_recv()
        if k == local - 1:
            @pl.when(x == 1)
            def _():
                gs[:, :, seq_rows(plane, k, 0), :] += block[local, 1]

            @pl.when(x == 0)
            def _():
                head_copies()[0][1].wait_recv()
                gs[:, :, seq_rows(plane, k, 0), :] += hx[...]

            @pl.when(above)
            def _():
                head_copies()[1][1].wait_recv()
                gs[:, :, seq_rows(plane, k, 1), :] += hz[...]
        if planes > 1:
            for kind in kinds:
                for way in ways:
                    z_start(way, 0, kind, k, 1)

    def take(step, kind, group):
        for way in ways:
            data = z_data(block_plane(way, step + 1), kind, 2 * group, 2)
            await_all(data, zrecv.at[way, kind, step, group], taking(way, step, kind))

    whole_groups = groups - 1 if last_step >= 2 else groups

    def pass_on(step, group, only=kinds):
        if planes > 1 and step <= last_step:
            for kind in only:
                if kind or step < 2:
                    take(step, kind, group)
                if step < last_step and (kind or step + 1 < 2):
                    split = step + 1 == last_step and last_step >= 2
                    for way in ways:
                        if not split or group < whole_groups:
                            z_start(way, step + 1, kind, 2 * group, 2)
                    if split and group == groups - 1:
                        for part in tail_parts:
                            for way in ways:
                                z_start(way, step + 1, kind, 2 * whole_groups,
                                        local - 2 * whole_groups, part)

    def take_last(part):
        first = 2 * whole_groups
        for way in ways:
            at = block_plane(way, last_step + 1)
            data = gs.at[part, :, seq_rows(at, first, 0, 2 * (local - first)), :]
            await_all(data, zlast.at[way, part], taking(way, last_step))

    def make_mats(target, rows, lanes, value):
        high, low = halves(value)
        count = 2 * store_rows
        target[pl.ds(rows * store_rows, store_rows), lanes] = high
        target[pl.ds(count + rows * store_rows, store_rows), lanes] = low

    def score(target, at, part):
        lines = []
        for line in range(8):
            first = at * in_plane * 8 + line
            for tile in range(tiles):
                lines.append(gs[part, tile, pl.ds(first, in_plane, stride=8), :])
        high, low = halves(jnp.concatenate(lines, axis=1))
        return times_t(
            jnp.concatenate([high, low], axis=0),
            target[:, pl.ds(part * part_lanes, part_lanes)],
        )

    def score_plane(at):
        value = score(mats, at, pushed)
        for part in range(pushed + 1, quarters):
            value += score(mats, at, part)
        sc[at] = value

        def more():
            value = score(mats, at, 0)
            for part in range(1, pushed):
                value += score(mats, at, part)
            sc[at] += value

        if pushed:
            when(no(outer), more)

    def score_guests():
        for step in range(2):
            await_all(guest.at[step], srecv.at[2 + step])
        lanes = pl.ds(0, pushed * part_lanes)
        for step in range(2):
            make_mats(guest_mats, step, lanes, guest[step])
        for at in range(planes):
            value = score(guest_mats, at, 0)
            for part in range(1, pushed):
                value += score(guest_mats, at, part)
            guest_sc[at] = value

    def score_step(step):
        for way in ways:
            when(taking(way, step), lambda way=way: score_plane(block_plane(way, step + 1)))

    def stage_rows(k):
        if 0 <= k < local:
            finish_rows(k)

    def stage_grads(k):
        if 0 <= k < local:
            gradients(k)
            if k % 2 and 1 < k < local - 2:
                trade(1)

    def stage_complete(k):
        if 0 <= k < local:
            complete(k)

    fold_left()
    project_out(0)
    pl.semaphore_wait(barrier, met)
    send_left(0)
    if pushed:
        push_own()
    trade(3)
    early = min(2, local) if blocks >= 3 else 0
    for b in range(blocks):
        chunks = range(b * span, b * span + span)
        if b == 0:
            for k in chunks:
                pair_left(k)
        project_in(b)
        send_right(b)
        if b:
            for k in chunks:
                pair_left(k)
        if b == blocks - 2 and early:
            stage_rows(0)
        if b + 1 < blocks:
            project_out(b + 1)
            send_left(b + 1)
        else:
            fetch("kept", stored.at[:, column(x, 0, pieces)], kept)
            if early:
                stage_grads(1)
        for k in chunks:
            pair_right(k)
        if b == blocks - 2 and early:
            stage_grads(0)
            stage_rows(1)
    passed = 0
    for k in range(early, local):
        stage_rows(k)
        stage_complete(k - 3)
        stage_grads(k)
        if k >= 5 and k % 2 and k < local - 1:
            pass_on(0, (k - 5) // 2)
            passed = (k - 5) // 2 + 1
    trade(pieces)
    trades_sent()
    rows_sent()
    stage_complete(local - 3)
    loads["kept"].wait()
    make_mats(mats, 0, pl.ds(0, half_lanes), kept[...])
    stage_complete(local - 2)
    stage_complete(local - 1)
    for group in range(passed, groups - 2):
        pass_on(0, group)
    passed = max(passed, groups - 2)
    for n in range(batches):
        push_given(n)
    pass_on(1, 0, (1,))

    loads["slots"].wait()
    at_row = lax.broadcasted_iota(jnp.int32, (seqs, seqs), 1)
    seq_of = ((at_row // in_plane) * 2 + at_row % 2) * local + (at_row % in_plane) // 2
    by_seq = jnp.where(lax.broadcasted_iota(jnp.int32, (seqs, seqs), 0) == seq_of, 1.0, 0.0)
    by_seq = by_seq.astype(BF16)
    slot = lax.broadcasted_iota(jnp.int32, (seqs, seqs), 0)
    by_slot = times(
        jnp.where(slots[...] == slot, 1.0, 0.0).astype(BF16), by_seq)
    row = lax.broadcasted_iota(jnp.int32, (4 * local, seqs), 0)
    wanted = jnp.zeros((4 * local, seqs), jnp.int32)
    for n, owner in enumerate((tok, beside, partner * 2 + x, partner * 2 + 1 - x)):
        here = (row >= n * local) & (row < (n + 1) * local)
        wanted = jnp.where(here, owner * local + row - n * local, wanted)
    pick = times(
        jnp.where(slots[...] == wanted, 1.0, 0.0).astype(BF16), by_seq).astype(BF16)
    pick = jnp.concatenate([pick, pick], axis=1)

    for group in range(passed, groups):
        pass_on(0, group)
        pass_on(1, group - 1, (1,))

    def given_mats(first, count):
        lanes = pl.ds(first * part_lanes, count * part_lanes)
        make_mats(mats, 1, lanes, given[:, lanes])

    def give(part, n, to, condition):
        lane = part * part_lanes
        there = pl.ds(pl.multiple_of(x * half_lanes + lane, part_lanes), part_lanes)
        sem = psent.at[n, 0 if part < pushed else 1]
        copies["p", n, part] = start(remote(
            picked.at[n, :, pl.ds(lane, part_lanes)], out.at[:, there],
            (sem, precv.at[n, part]), to, feat), condition)

    def fill_rows(part):
        count = 4 if part < pushed else 2
        for line in range(8):
            high, low = halves(jnp.concatenate(
                [gs[part, tile, pl.ds(line, seqs, stride=8), :] for tile in range(tiles)], axis=1))
            taken = times(pick[: count * local], jnp.concatenate([high, low], axis=0))
            lane = part * part_lanes + line * rank
            out[:, pl.ds(pl.multiple_of(x * half_lanes + lane, rank), rank)] = taken[:local]
            for n in range(1, count):
                picked[n - 1, :, pl.ds(lane, rank)] = taken[n * local : (n + 1) * local]

    def hand_rows(part, condition):
        if part < pushed:
            give(part, 1, partner * 2 + x, inner)
            give(part, 2, partner * 2 + 1 - x, inner)
        give(part, 0, beside, condition)

    def rows_for_slots(part):
        condition = no(outer) if part < pushed else True
        when(condition, lambda: fill_rows(part))
        hand_rows(part, condition)

    def turn_scores(sums):
        count = 2 * store_rows
        high, low = sums[:, :in_plane], sums[:, in_plane:]
        by_row = (high[:, :, :count] + high[:, :, count:] + low[:, :, :count]).reshape(seqs, count)
        lanes = scored.shape[4]
        placed = jnp.dot(
            by_slot, by_row, precision=lax.Precision.HIGHEST, preferred_element_type=F32)
        if lanes > seqs:
            placed = jnp.concatenate([placed, jnp.zeros((lanes - seqs, count), F32)], axis=0)
        return jnp.transpose(
            jnp.concatenate([placed, jnp.zeros((lanes, 128 - count), F32)], axis=1))

    few = scored.shape[3]
    parts = {}

    def send_scores(kind, own, condition):
        base = partner if kind else plane
        for step in range(2):
            for turn in range(feats):
                if kind or step or turn:
                    to = (feat + turn) % feats
                    parts[kind, step, turn] = start(remote(
                        scored.at[kind, step, to], landed.at[kind, step * feats + turn],
                        (rsent.at[kind], rrecv.at[kind]),
                        base * 2 + (1 - x if step else x), to,
                    ), condition)
        first = 0 if kind else 1
        await_sent(landed.at[kind, pl.ds(first, 2 * feats - first)], rsent.at[kind], condition)

    def place_scores(kind, sums):
        turned = turn_scores(sums)
        for step in range(2):
            for f in range(feats):
                first = (step * feats + f) * few
                scored[kind, step, f] = turned[first : first + few]

    def share_guests():
        when(inner, lambda: place_scores(1, guest_sc[...]))
        send_scores(1, guest_sc, inner)

    def share_scores():
        place_scores(0, sc[...])
        send_scores(0, sc, True)

    if pushed:
        for group in range(groups):
            pass_on(1, group, (0,))
        pass_on(1, groups - 1, (1,))
        for part in range(pushed):
            rows_for_slots(part)
        when(inner, score_guests)
        share_guests()
        when(inner, lambda: [fill_rows(part) for part in tail_parts] and None)
        for part in tail_parts:
            hand_rows(part, inner)
    else:
        pass_on(1, groups - 1, (1,))
    for n in range(batches):
        await_all(given.at[:, batch_lanes(n)], srecv.at[4 + n], no(outer))
    await_all(given.at[:, pl.ds(aside * piece, (pieces - aside) * piece)], srecv.at[1])
    given_mats(pushed, quarters - pushed)
    if pushed:
        when(no(outer), lambda: given_mats(0, pushed))
    score_plane(plane)
    score_step(0)
    if last_step > 0:
        score_step(1)
    for step in range(2, last_step + 1):
        for group in range(groups if step < last_step else whole_groups):
            pass_on(step, group)
        if step < last_step:
            score_step(step)
    for part in tail_parts:
        if last_step >= 2:
            take_last(part)
        if pushed:
            when(outer, lambda part=part: fill_rows(part))
            hand_rows(part, outer)
        else:
            rows_for_slots(part)
    if last_step >= 2:
        score_step(last_step)

    def sum_scores():
        others = pl.ds(1, 2 * feats - 1)
        await_all(landed.at[0, others], rrecv.at[0])
        summed = scored[0, 0, feat]
        for n in range(1, 2 * feats):
            summed += landed[0, n]
        total[...] = summed[:, :seqs]

        def add_more():
            await_all(landed.at[1], rrecv.at[1])
            more = landed[1, 0]
            for n in range(1, 2 * feats):
                more += landed[1, n]
            total[...] += more[:, :seqs]

        if pushed:
            when(outer, add_more)

    def drain():
        for part in range(quarters):
            arrives = no(outer) if part < pushed else True
            when(arrives, copies["p", 0, part].wait_recv)
        for part in range(pushed):
            for n in (1, 2):
                when(outer, copies["p", n, part].wait_recv)
        sum_scores()
        if planes > 1:
            z_sent()
        for kind, first, count in ((0, 0, pushed), (1, pushed, quarters - pushed)):
            lanes = pl.ds(first * part_lanes, count * part_lanes)
            if count:
                await_sent(picked.at[0, :, lanes], psent.at[0, kind], True if kind else no(outer))
                for n in (1, 2):
                    if not kind:
                        await_sent(picked.at[n, :, lanes], psent.at[n, kind], inner)
        for condition, copy in sent:
            when(condition, copy.wait_send)
        for condition, copy in head_copies():
            when(condition, copy.wait_send)

    share_scores()
    drain()


def body(
    activations,
    out_grads,
    proj_in,
    proj_out,
    left_factor,
    right_factor,
    seq_lengths,
    seq_slots,
    stored_grads,
):
    dma = pltpu.SemaphoreType.DMA
    feats, toks = lax.axis_size("feat"), lax.axis_size("tok")
    rank = right_factor.shape[0]
    tok_rows = activations.shape[0]
    seqs = seq_lengths.shape[0]
    local = seqs // toks
    chunk = tok_rows // local
    store_rows, width = stored_grads.shape
    planes, chips = toks // 2, feats // 2
    wide = rank // feats
    quarters = wide // 16
    tiles = rank // 128
    score_rows = store_rows // feats
    lanes = seqs + -seqs % 128
    half = chunk // 2
    steps = max(planes - 1, 1)
    pieces = width // 2 // (2 * rank)
    pushed = pushed_quarters(planes, quarters)
    aside = max(pushed, 1)
    aside_lanes = aside * 8 * rank

    def vmem(*shape, dtype=F32):
        return pltpu.VMEM(shape, dtype)

    scores, own_rows = pl.pallas_call(
        functools.partial(kernel, (toks, feats, local, chunk, rank, seqs, store_rows)),
        out_shape=[
            pltpu.VMEM((score_rows, seqs), F32),
            pltpu.VMEM((local, width), F32),
        ],
        in_specs=[ANY] * 9,
        out_specs=[VMEM, VMEM],
        scratch_shapes=[
            vmem(*out_grads.shape, dtype=BF16),
            vmem(*activations.shape, dtype=BF16),
            vmem(*proj_out.shape, dtype=BF16),
            vmem(*proj_in.shape, dtype=BF16),
            vmem(rank, rank),
            vmem(rank, rank),
            vmem(1, seqs, dtype=jnp.int32),
            vmem(1, seqs, dtype=jnp.int32),
            vmem(2, rank, rank, dtype=BF16),
            vmem(3 * rank, rank, dtype=BF16),
            vmem(2, *proj_out.shape, dtype=BF16),
            vmem(local, 2, chips, wide, chunk),
            vmem(local, chips, wide, chunk),
            vmem(local, chips, wide, chunk),
            vmem(local, chips - 1, wide, chunk),
            vmem(local, wide, chunk),
            vmem(local, 2, half, rank),
            vmem(local, half, rank),
            vmem(local, half, rank),
            vmem(local, chips - 1, half, rank),
            vmem(local, 2, half, rank),
            vmem(local + 1, 2, quarters, tiles, 8, 128),
            vmem(quarters, tiles, 8, 128),
            vmem(quarters, tiles, 8, 128),
            vmem(quarters, tiles, seqs * 8, 128),
            vmem(store_rows, width // 2),
            vmem(store_rows, width // 2),
            vmem(2, store_rows, aside_lanes),
            vmem(4 * store_rows, width // 2, dtype=BF16),
            vmem(4 * store_rows, aside_lanes, dtype=BF16),
            vmem(planes, 4 * local, 4 * store_rows),
            vmem(planes, 4 * local, 4 * store_rows),
            vmem(3, local, width // 2),
            vmem(2, 2, feats, score_rows, lanes),
            vmem(2, 2 * feats, score_rows, lanes),
            dma((2 * (local // 2 if local % 2 == 0 else local) + 7,)),
            dma((2, local)),
            dma((2, local, chips - 1)),
            dma((local,)),
            dma((local,)),
            dma((2,)),
            dma((2, 2, steps, (local + 1) // 2)),
            dma((2, quarters)),
            dma((8,)),
            dma((3, quarters)),
            dma((2,)),
            dma((2,)),
            dma((2, chips - 1)),
            dma((1,)),
            dma((1,)),
            dma((3,)),
            dma((2, 2, steps)),
            dma((4,)),
            dma((3, 2)),
            dma((2,)),
        ],
        compiler_params=pltpu.CompilerParams(
            collective_id=0, has_side_effects=True, vmem_limit_bytes=60 << 20
        ),
        name="influence",
    )(
        out_grads, activations, proj_out, proj_in, left_factor, right_factor,
        seq_lengths.reshape(1, seqs), seq_slots.reshape(1, seqs), stored_grads,
    )
    return scores, own_rows


def solution(mesh):
    placed = (
        P("tok", "feat"),
        P("tok", "feat"),
        P("feat", None),
        P("feat", None),
        P(),
        P(),
        P(),
        P(),
        P("tok", "feat"),
    )
    return jax.shard_map(
        body,
        mesh=mesh,
        in_specs=placed,
        out_specs=(P(("tok", "feat"), None), P("tok", "feat")),
        check_vma=False,
    )
```

```python
import functools

import jax
import jax.numpy as jnp
from jax import lax
from jax.experimental import pallas as pl
from jax.experimental.pallas import tpu as pltpu
from jax.sharding import PartitionSpec as P

MESH = pl.DeviceIdType.MESH
VMEM = pl.BlockSpec(memory_space=pltpu.VMEM)
ANY = pl.BlockSpec(memory_space=pl.ANY)
F32, BF16 = jnp.float32, jnp.bfloat16
DOWN, UP = 0, 1


def halves(value):
    high = value.astype(BF16)
    return high, (value - high.astype(F32)).astype(BF16)


def times(left, right):
    return jnp.dot(left, right, preferred_element_type=F32)


def times_t(left, right):
    return lax.dot_general(left, right, (((1,), (1,)), ((), ())), preferred_element_type=F32)


def stack_left(value, axis):
    high, low = halves(value)
    return jnp.concatenate([high, low, high], axis=axis)


def stack_right(value, axis):
    high, low = halves(value)
    return jnp.concatenate([high, high, low], axis=axis)


def aligned(index, size):
    return pl.ds(pl.multiple_of(index * size, size), size)


def pushed_quarters(planes, quarters):
    return quarters // 2 if planes == 4 else 0


def both(first, second):
    if first is True:
        return second
    if second is True:
        return first
    return False if first is False or second is False else first & second


def no(value):
    return not value if isinstance(value, bool) else jnp.logical_not(value)


def when(condition, action):
    if condition is True:
        action()
    elif condition is not False:
        pl.when(condition)(action)


def kernel(dims, *refs):
    toks, feats, local, chunk, rank, seqs, store_rows = dims
    out_rows, in_rows, out_mat, in_mat, left_hbm, right_hbm, lens_hbm, slots_hbm, stored = refs[:9]
    total, out = refs[9:11]
    lhs_o, lhs_i, rhs_o, rhs_i, left_f, right_f, lens, slots = refs[11:19]
    left_cat, right_cat, folded = refs[19:22]
    lp, la, ly, lb, lfin = refs[22:27]
    rp, ra, ry, rb, rfull = refs[27:32]
    block, hx, hz, gs = refs[32:36]
    kept, given, guest, mats, guest_mats, sc, guest_sc = refs[36:43]
    picked, scored, landed = refs[43:46]
    load, asem, bsem, csem, xsem, hsem, zpushed, zkept, zlast, srecv, precv, rrecv = refs[46:58]
    asent, bsent, csent, xsent, hsent, zsent, ssent, psent, rsent = refs[58:]

    tok, feat = lax.axis_index("tok"), lax.axis_index("feat")
    plane, x = tok // 2, tok % 2
    y, c = feat // 2, feat % 2
    planes = toks // 2
    mate, chips = feat + 1 - 2 * c, feats // 2
    across = [(y + turn) % chips for turn in range(1, chips)]
    beside = tok + 1 - 2 * x
    wide = rank // feats
    half_o = wide // 2
    quarters = half_o // 8
    in_plane = 2 * local
    half_lanes = half_o * rank
    part_lanes = 8 * rank
    tiles = rank // 128
    below, above = plane > 0, plane < planes - 1
    pushed = pushed_quarters(planes, quarters)
    outer = inner = False
    if pushed:
        outer = (plane == 0) | (plane == planes - 1)
        inner = (plane == 1) | (plane == planes - 2)
    partner = jnp.where(plane == 0, 1, jnp.where(
        plane == planes - 1, planes - 2, jnp.where(plane == 1, 0, planes - 1)))

    def remote(src, dst, sems, to_tok, to_feat):
        return pltpu.make_async_remote_copy(
            src_ref=src, dst_ref=dst, send_sem=sems[0], recv_sem=sems[1],
            device_id=(to_tok, to_feat), device_id_type=MESH,
        )

    loads = {}
    span = 2 if local % 2 == 0 else 1
    blocks = local // span
    tall = span * chunk

    def fetch(key, src, dst):
        loads[key] = pltpu.make_async_copy(src, dst, load.at[len(loads)])
        loads[key].start()

    def fetch_block(b):
        if b < blocks:
            rows = pl.ds(b * tall, tall)
            if b:
                fetch(("o", b), out_rows.at[rows], lhs_o.at[rows])
            fetch(("i", b), in_rows.at[rows], lhs_i.at[rows])

    fetch("left", left_hbm, left_f)
    fetch("out", out_mat, rhs_o)
    fetch(("o", 0), out_rows.at[pl.ds(0, tall)], lhs_o.at[pl.ds(0, tall)])
    fetch("in", in_mat, rhs_i)
    fetch_block(0)
    fetch("lens", lens_hbm, lens)
    fetch("slots", slots_hbm, slots)
    fetch("right", right_hbm, right_f)

    barrier = pltpu.get_barrier_semaphore()

    def greet(to_tok, to_feat):
        pl.semaphore_signal(barrier, inc=1, device_id=(to_tok, to_feat), device_id_type=MESH)

    for step in range(2):
        for turn in range(feats):
            if step or turn:
                greet(beside if step else tok, (feat + turn) % feats)
    met = 2 * feats - 1
    for side, there, crossing in ((-1, below, 0), (1, above, 1)):
        near = False
        if pushed:
            near = (outer & (partner == plane + side)) | (inner & (partner == plane + side))
        plain = both(there, no(near))
        corner = both(plain, x == crossing)
        met += plain.astype(jnp.int32) + corner.astype(jnp.int32)

        def greet_all(side=side):
            for other in range(2):
                for f in range(feats):
                    greet((plane + side) * 2 + other, f)

        if pushed:
            met += 2 * feats * near.astype(jnp.int32)
        when(near, greet_all)
        when(plain, lambda side=side: greet(tok + 2 * side, feat))
        when(corner, lambda side=side: greet(tok + side, feat))

    sent = []

    def start(copy, condition=True):
        when(condition, copy.start)
        return copy

    def await_sent(src, sem, condition=True):
        copy = remote(src, src, (sem, sem), tok, mate)
        sent.append((condition, copy))

    def await_all(dst, sem, condition=True):
        copy = remote(dst, dst, (sem, sem), tok, mate)
        when(condition, copy.wait_recv)

    piece = 2 * rank
    pieces = half_lanes // piece
    aside = pushed * part_lanes // piece
    trades = []

    def column(half, first, count=1):
        lanes = half * half_lanes + first * piece
        return pl.ds(pl.multiple_of(lanes, piece), piece * count)

    def push_own():
        copy = remote(
            stored.at[:, column(x, 0, aside)], guest.at[0], (ssent.at[2], srecv.at[2]),
            partner * 2 + x, feat)
        start(copy, outer)
        await_sent(stored.at[:, column(x, 0, aside)], ssent.at[2], outer)

    batches = 4 if pushed else 0
    batch = aside // 4

    def batch_lanes(n):
        return pl.ds(n * batch * piece, batch * piece)

    def push_given(n):
        lanes = batch_lanes(n)
        await_all(given.at[:, lanes], srecv.at[4 + n], outer)
        start(remote(
            given.at[:, lanes], guest.at[1, :, lanes], (ssent.at[3], srecv.at[3]),
            partner * 2 + x, feat), outer)

    def trade(count):
        for _ in range(count):
            n = len(trades)
            if n < pieces:
                kind = 0 if n < aside else 1
                trades.append(start(remote(
                    stored.at[:, column(1 - x, n)], given.at[:, pl.ds(n * piece, piece)],
                    (ssent.at[kind], srecv.at[1 if kind else 4 + n // batch]), beside, feat,
                )))

    def trades_sent():
        if aside:
            await_sent(stored.at[:, column(1 - x, 0, aside)], ssent.at[0])
            await_sent(given.at[:, pl.ds(0, aside * piece)], ssent.at[3], outer)
        await_sent(stored.at[:, column(1 - x, aside, pieces - aside)], ssent.at[1])

    copies = {}

    def fold_left():
        loads["left"].wait()
        for core in range(2):
            for side in range(chips):
                rows = left_f[pl.ds((side * 2 + core) * wide, wide), :]
                high, low = halves(rows)
                left_cat[0, pl.ds((core * chips + side) * wide, wide), :] = high
                left_cat[1, pl.ds((core * chips + side) * wide, wide), :] = low
        loads["out"].wait()
        depth = rhs_o.shape[0]
        step = min(256, depth)
        for n in range(depth // step):
            rows = rhs_o[pl.ds(n * step, step), :]
            folded[0, pl.ds(n * step, step), :], folded[1, pl.ds(n * step, step), :] = halves(
                times_t(rows, left_cat[0]) + times_t(rows, left_cat[1]))

    def project_out(b):
        loads["o", b].wait()
        own = [lhs_o[pl.ds((b * span + n) * chunk, chunk), :] for n in range(span)]
        sums = [times(rows, folded[0]) + times(rows, folded[1]) for rows in own]
        for n in range(span):
            lp[b * span + n] = jnp.transpose(sums[n]).reshape(2, chips, wide, chunk)

    def send_left(b):
        for k in range(b * span, b * span + span):
            copies["a", 0, k] = start(remote(
                lp.at[k, 1 - c], la.at[k], (asent.at[0], asem.at[0, b]), tok, mate))

    def pair_left(k):
        if k % span == 0:
            await_all(la.at[pl.ds(k, span)], asem.at[0, k // span])
        ly[k] = lp[k, c] + la[k]
        for n, other in enumerate(across):
            copies["b", 0, k, n] = start(remote(
                ly.at[k, other], lb.at[k, n], (bsent.at[0, n], bsem.at[0, k, n]),
                tok, other * 2 + c))

    def project_in(b):
        if b == 0:
            loads["in"].wait()
        loads["i", b].wait()
        if b == 0:
            fetch_block(1)
        fetch_block(b + 2)
        own = [lhs_i[pl.ds((b * span + n) * chunk, chunk), :] for n in range(span)]
        for n, sums in enumerate([times(rows, rhs_i[...]) for rows in own]):
            rp[b * span + n] = sums.reshape(2, chunk // 2, rank)

    def send_right(b):
        for k in range(b * span, b * span + span):
            copies["a", 1, k] = start(remote(
                rp.at[k, 1 - c], ra.at[k], (asent.at[1], asem.at[1, b]), tok, mate))

    def pair_right(k):
        if k % span == 0:
            await_all(ra.at[pl.ds(k, span)], asem.at[1, k // span])
        ry[k] = rp[k, c] + ra[k]
        for n, other in enumerate(across):
            copies["b", 1, k, n] = start(remote(
                ry.at[k], rb.at[k, n], (bsent.at[1, n], bsem.at[1, k, n]),
                tok, other * 2 + c))

    def rows_sent():
        for side, ref in ((0, lp), (1, rp)):
            await_sent(ref.at[:, 1 - c], asent.at[side])
        for n, other in enumerate(across):
            await_sent(ly.at[:, other], bsent.at[0, n])
            await_sent(ry, bsent.at[1, n])
        await_sent(rfull.at[:, c], csent.at[0])
        await_sent(block.at[pl.ds(0, local), 1 - x], xsent.at[0])

    def finish_rows(k):
        if k == 0:
            loads["right"].wait()
            right_cat[...] = stack_right(right_f[...], 0)
        left, rows = ly[k, y], ry[k]
        for n in range(chips - 1):
            copies["b", 0, k, n].wait_recv()
            left += lb[k, n]
        lfin[k] = left
        for n in range(chips - 1):
            copies["b", 1, k, n].wait_recv()
            rows += rb[k, n]
        rfull[k, c] = times(stack_left(rows, 1), right_cat[...])
        copies["c", k] = start(remote(
            rfull.at[k, c], rfull.at[k, c], (csent.at[0], csem.at[k]), tok, mate))

    spans = {}

    def starts_of():
        loads["lens"].wait()
        lengths = lens[...].astype(F32)
        number = lax.broadcasted_iota(jnp.int32, (local, seqs), 1)
        mine = lax.broadcasted_iota(jnp.int32, (local, seqs), 0) + tok * local

        def pick(mask):
            return jnp.sum(jnp.where(mask, lengths, 0.0), axis=1, keepdims=True)

        spans["start"] = pick(number < mine)
        spans["now"] = 1.0 / jnp.maximum(pick(number == mine), 1.0)
        spans["before"] = 1.0 / jnp.maximum(pick(number == mine - 1), 1.0)

    def seq_rows(at_plane, number, side, count=1):
        first = (at_plane * in_plane + number * 2 + side) * 8
        return pl.ds(pl.multiple_of(first, 8), 8 * count)

    def settle(k, value):
        for tile in range(tiles):
            part = value[:, tile * 128 : (tile + 1) * 128]
            block[k, :, :, tile] = part.reshape(2, quarters, 8, 128)
        if k < local:
            gs[:, :, seq_rows(plane, k, x), :] = block[k, x]
            copies["x", k] = start(remote(
                block.at[k, 1 - x], gs.at[:, :, seq_rows(plane, k, x), :],
                (xsent.at[0], xsem.at[k]), beside, feat))
            if k < local - 1:
                z_own(k, x)

    def head_copies():
        return (
            (x == 1, remote(block.at[local, 0], hx, (hsent.at[0], hsem.at[0]), beside, feat)),
            ((x == 0) & below, remote(
                block.at[local, 0], hz, (hsent.at[1], hsem.at[1]), tok - 2, feat)),
            ((x == 0) & below, remote(
                block.at[local, 1], hz, (hsent.at[2], hsem.at[1]), tok - 1, feat)),
        )

    carry = {}

    def gradients(k):
        if k == 0:
            starts_of()
        copies["c", k].wait_recv()
        places = lax.broadcasted_iota(jnp.int32, (1, chunk), 1) + (tok * local + k) * chunk
        inside = places.astype(F32) >= spans["start"][k : k + 1]
        now = jnp.where(inside, spans["now"][k : k + 1], 0.0)
        before = jnp.where(inside, 0.0, spans["before"][k : k + 1])
        left = lfin[k]
        weighted = jnp.concatenate([left * now, left * before], axis=0)
        right = rfull[k].reshape(chunk, rank)
        both = times(stack_left(weighted, 1), stack_right(right, 0))
        tail = both[wide:]
        if k:
            settle(k - 1, carry["sum"] + tail)
        else:
            settle(local, tail)
            for condition, copy in head_copies():
                when(condition, copy.start)
        carry["sum"] = both[:wide]
        if k == local - 1:
            settle(k, carry["sum"])

    ways = (DOWN, UP)

    def block_plane(way, step):
        return jnp.clip(plane + step if way == DOWN else plane - step, 0, planes - 1)

    def to_outer(way):
        return (plane == 1 if way == DOWN else plane == planes - 2) if pushed else False

    def sending(way, step, kind=1):
        if way == DOWN:
            base = below & (plane + step < planes)
        else:
            base = above & (plane - step >= 0)
        return base if kind else both(base, no(to_outer(way)))

    def taking(way, step, kind=1):
        base = plane + 1 + step < planes if way == DOWN else plane - 1 - step >= 0
        return base if kind else both(base, no(outer))

    groups = local // 2
    tail_parts = range(pushed, quarters)
    kinds = (0, 1) if pushed else (1,)

    def z_data(at, kind, first, count):
        which = pl.ds(pushed, quarters - pushed) if kind else pl.ds(0, pushed)
        return gs.at[which, :, seq_rows(at, first, 0, 2 * count), :]

    def z_start(way, step, kind, first, count, part=None):
        data = z_data(block_plane(way, step), kind, first, count)
        came = came_by(way, kind, step, first // 2)
        if part is not None:
            data = gs.at[part, :, seq_rows(block_plane(way, step), first, 0, 2 * count), :]
            came = zlast.at[way, part]
        copy = remote(
            data, data, (zsent.at[way, kind, step], came),
            tok - 2 if way == DOWN else tok + 2, feat)
        when(sending(way, step, kind), copy.start)

    def came_by(way, kind, step, group):
        if kind:
            return zkept.at[way, step, group]
        return zpushed.at[way, groups if step else group]

    def take_pushed():
        for way in ways:
            data = z_data(block_plane(way, 2), 0, 0, local)
            await_all(data, came_by(way, 0, 1, 0), taking(way, 1, 0))

    def z_own(number, side):
        if planes > 1:
            for kind in kinds:
                which = pl.ds(pushed, quarters - pushed) if kind else pl.ds(0, pushed)
                data = gs.at[which, :, seq_rows(plane, number, side), :]
                for way in ways:
                    copy = remote(
                        data, data, (zsent.at[way, kind, 0], came_by(way, kind, 0, number // 2)),
                        tok - 2 if way == DOWN else tok + 2, feat)
                    when(sending(way, 0, kind), copy.start)

    def z_sent():
        for step in range(last_step + 1):
            for way in ways:
                for kind in kinds:
                    if kind or step < 2:
                        data = z_data(block_plane(way, step), kind, 0, local)
                        await_sent(data, zsent.at[way, kind, step], sending(way, step, kind))

    last_step = max(planes - 2, 0)

    def complete(k):
        copies["x", k].wait_recv()
        if k == local - 1:
            @pl.when(x == 1)
            def _():
                gs[:, :, seq_rows(plane, k, 0), :] += block[local, 1]

            @pl.when(x == 0)
            def _():
                head_copies()[0][1].wait_recv()
                gs[:, :, seq_rows(plane, k, 0), :] += hx[...]

            @pl.when(above)
            def _():
                head_copies()[1][1].wait_recv()
                gs[:, :, seq_rows(plane, k, 1), :] += hz[...]
        z_own(k, 1 - x)
        if k == local - 1:
            z_own(k, x)

    def take(step, kind, group):
        for way in ways:
            data = z_data(block_plane(way, step + 1), kind, 2 * group, 2)
            await_all(data, came_by(way, kind, step, group), taking(way, step, kind))

    whole_groups = groups - 1 if last_step >= 2 else groups

    def pass_on(step, group, only=kinds):
        if planes > 1 and step <= last_step:
            for kind in only:
                if kind or step < 2:
                    take(step, kind, group)
                if step < last_step and (kind or step + 1 < 2):
                    split = step + 1 == last_step and last_step >= 2
                    for way in ways:
                        if not split or group < whole_groups:
                            z_start(way, step + 1, kind, 2 * group, 2)
                    if split and group == groups - 1:
                        for part in tail_parts:
                            for way in ways:
                                z_start(way, step + 1, kind, 2 * whole_groups,
                                        local - 2 * whole_groups, part)

    def take_last(part):
        first = 2 * whole_groups
        for way in ways:
            at = block_plane(way, last_step + 1)
            data = gs.at[part, :, seq_rows(at, first, 0, 2 * (local - first)), :]
            await_all(data, zlast.at[way, part], taking(way, last_step))

    def make_mats(target, rows, lanes, value):
        high, low = halves(value)
        count = 2 * store_rows
        target[pl.ds(rows * store_rows, store_rows), lanes] = high
        target[pl.ds(count + rows * store_rows, store_rows), lanes] = low

    def score(target, at, part):
        lines = []
        for line in range(8):
            first = at * in_plane * 8 + line
            for tile in range(tiles):
                lines.append(gs[part, tile, pl.ds(first, in_plane, stride=8), :])
        high, low = halves(jnp.concatenate(lines, axis=1))
        return times_t(
            jnp.concatenate([high, low], axis=0),
            target[:, pl.ds(part * part_lanes, part_lanes)],
        )

    def score_plane(at):
        value = score(mats, at, pushed)
        for part in range(pushed + 1, quarters):
            value += score(mats, at, part)
        sc[at] = value

        def more():
            value = score(mats, at, 0)
            for part in range(1, pushed):
                value += score(mats, at, part)
            sc[at] += value

        if pushed:
            when(no(outer), more)

    def score_guests():
        for step in range(2):
            await_all(guest.at[step], srecv.at[2 + step])
        lanes = pl.ds(0, pushed * part_lanes)
        for step in range(2):
            make_mats(guest_mats, step, lanes, guest[step])
        for at in range(planes):
            value = score(guest_mats, at, 0)
            for part in range(1, pushed):
                value += score(guest_mats, at, part)
            guest_sc[at] = value

    def score_step(step):
        for way in ways:
            when(taking(way, step), lambda way=way: score_plane(block_plane(way, step + 1)))

    def stage_rows(k):
        if 0 <= k < local:
            finish_rows(k)

    def stage_grads(k):
        if 0 <= k < local:
            gradients(k)
            if k == 3:
                trade(1)

    def stage_complete(k):
        if 0 <= k < local:
            complete(k)

    fold_left()
    project_out(0)
    pl.semaphore_wait(barrier, met)
    send_left(0)
    if pushed:
        push_own()
    trade(3)
    early = min(2, local) if blocks >= 3 else 0
    for b in range(blocks):
        chunks = range(b * span, b * span + span)
        if b == 0:
            for k in chunks:
                pair_left(k)
        project_in(b)
        send_right(b)
        if b:
            for k in chunks:
                pair_left(k)
        if b == 1:
            trade(2)
        if b == blocks - 2 and early:
            stage_rows(0)
        if b + 1 < blocks:
            project_out(b + 1)
            send_left(b + 1)
        else:
            fetch("kept", stored.at[:, column(x, 0, pieces)], kept)
            if early:
                stage_grads(1)
        for k in chunks:
            pair_right(k)
        if b == blocks - 2 and early:
            stage_grads(0)
            stage_rows(1)
    passed = 0
    for k in range(early, local):
        stage_rows(k)
        stage_complete(k - 3)
        stage_grads(k)
        if k >= 5 and k % 2 and k < local - 1:
            pass_on(0, (k - 5) // 2)
            passed = (k - 5) // 2 + 1
    trade(pieces)
    trades_sent()
    rows_sent()
    stage_complete(local - 3)
    loads["kept"].wait()
    make_mats(mats, 0, pl.ds(0, half_lanes), kept[...])
    stage_complete(local - 2)
    stage_complete(local - 1)
    for group in range(passed, groups - 2):
        pass_on(0, group)
    passed = max(passed, groups - 2)
    for n in range(batches):
        push_given(n)
    pass_on(1, 0, (1,))

    loads["slots"].wait()
    at_row = lax.broadcasted_iota(jnp.int32, (seqs, seqs), 1)
    seq_of = ((at_row // in_plane) * 2 + at_row % 2) * local + (at_row % in_plane) // 2
    by_seq = jnp.where(lax.broadcasted_iota(jnp.int32, (seqs, seqs), 0) == seq_of, 1.0, 0.0)
    by_seq = by_seq.astype(BF16)
    slot = lax.broadcasted_iota(jnp.int32, (seqs, seqs), 0)
    by_slot = times(
        jnp.where(slots[...] == slot, 1.0, 0.0).astype(BF16), by_seq)
    row = lax.broadcasted_iota(jnp.int32, (4 * local, seqs), 0)
    wanted = jnp.zeros((4 * local, seqs), jnp.int32)
    for n, owner in enumerate((tok, beside, partner * 2 + x, partner * 2 + 1 - x)):
        here = (row >= n * local) & (row < (n + 1) * local)
        wanted = jnp.where(here, owner * local + row - n * local, wanted)
    pick = times(
        jnp.where(slots[...] == wanted, 1.0, 0.0).astype(BF16), by_seq).astype(BF16)
    pick = jnp.concatenate([pick, pick], axis=1)

    for group in range(passed, groups):
        pass_on(0, group)
        pass_on(1, group - 1, (1,))

    def given_mats(first, count):
        lanes = pl.ds(first * part_lanes, count * part_lanes)
        make_mats(mats, 1, lanes, given[:, lanes])

    def give(part, n, to, condition):
        lane = part * part_lanes
        there = pl.ds(pl.multiple_of(x * half_lanes + lane, part_lanes), part_lanes)
        sem = psent.at[n, 0 if part < pushed else 1]
        copies["p", n, part] = start(remote(
            picked.at[n, :, pl.ds(lane, part_lanes)], out.at[:, there],
            (sem, precv.at[n, 0 if part < pushed else 1]), to, feat), condition)

    def fill_rows(part):
        count = 4 if part < pushed else 2
        for line in range(8):
            high, low = halves(jnp.concatenate(
                [gs[part, tile, pl.ds(line, seqs, stride=8), :] for tile in range(tiles)], axis=1))
            taken = times(pick[: count * local], jnp.concatenate([high, low], axis=0))
            lane = part * part_lanes + line * rank
            out[:, pl.ds(pl.multiple_of(x * half_lanes + lane, rank), rank)] = taken[:local]
            for n in range(1, count):
                picked[n - 1, :, pl.ds(lane, rank)] = taken[n * local : (n + 1) * local]

    def hand_rows(part, condition):
        if part < pushed:
            give(part, 2, partner * 2 + 1 - x, inner)
            give(part, 1, partner * 2 + x, inner)
        give(part, 0, beside, condition)

    def rows_for_slots(part):
        condition = no(outer) if part < pushed else True
        when(condition, lambda: fill_rows(part))
        hand_rows(part, condition)

    def turn_scores(sums):
        count = 2 * store_rows
        high, low = sums[:, :in_plane], sums[:, in_plane:]
        by_row = (high[:, :, :count] + high[:, :, count:] + low[:, :, :count]).reshape(seqs, count)
        lanes = scored.shape[4]
        placed = jnp.dot(
            by_slot, by_row, precision=lax.Precision.HIGHEST, preferred_element_type=F32)
        if lanes > seqs:
            placed = jnp.concatenate([placed, jnp.zeros((lanes - seqs, count), F32)], axis=0)
        return jnp.transpose(
            jnp.concatenate([placed, jnp.zeros((lanes, 128 - count), F32)], axis=1))

    few = scored.shape[3]
    parts = {}

    def send_scores(kind, own, condition):
        base = partner if kind else plane
        for step in range(2):
            for turn in range(feats):
                if kind or step or turn:
                    to = (feat + turn) % feats
                    parts[kind, step, turn] = start(remote(
                        scored.at[kind, step, to], landed.at[kind, step * feats + turn],
                        (rsent.at[kind], rrecv.at[kind]),
                        base * 2 + (1 - x if step else x), to,
                    ), condition)
        first = 0 if kind else 1
        await_sent(landed.at[kind, pl.ds(first, 2 * feats - first)], rsent.at[kind], condition)

    def place_scores(kind, sums):
        turned = turn_scores(sums)
        for step in range(2):
            for f in range(feats):
                first = (step * feats + f) * few
                scored[kind, step, f] = turned[first : first + few]

    def share_guests():
        when(inner, lambda: place_scores(1, guest_sc[...]))
        send_scores(1, guest_sc, inner)

    def share_scores():
        place_scores(0, sc[...])
        send_scores(0, sc, True)

    if pushed:
        take_pushed()
        pass_on(1, groups - 1, (1,))
        for part in range(pushed):
            rows_for_slots(part)
        when(inner, score_guests)
        share_guests()
        when(inner, lambda: [fill_rows(part) for part in tail_parts] and None)
        for part in tail_parts:
            hand_rows(part, inner)
    else:
        pass_on(1, groups - 1, (1,))
    for n in range(batches):
        await_all(given.at[:, batch_lanes(n)], srecv.at[4 + n], no(outer))
    await_all(given.at[:, pl.ds(aside * piece, (pieces - aside) * piece)], srecv.at[1])
    given_mats(pushed, quarters - pushed)
    if pushed:
        when(no(outer), lambda: given_mats(0, pushed))
    score_plane(plane)
    score_step(0)
    if last_step > 0:
        score_step(1)
    for step in range(2, last_step + 1):
        for group in range(groups if step < last_step else whole_groups):
            pass_on(step, group)
        if step < last_step:
            score_step(step)
    for part in tail_parts:
        if last_step >= 2:
            take_last(part)
        if pushed:
            when(outer, lambda part=part: fill_rows(part))
            hand_rows(part, outer)
        else:
            rows_for_slots(part)
    if last_step >= 2:
        score_step(last_step)

    def sum_scores():
        others = pl.ds(1, 2 * feats - 1)
        await_all(landed.at[0, others], rrecv.at[0])
        summed = scored[0, 0, feat]
        for n in range(1, 2 * feats):
            summed += landed[0, n]
        total[...] = summed[:, :seqs]

        def add_more():
            await_all(landed.at[1], rrecv.at[1])
            more = landed[1, 0]
            for n in range(1, 2 * feats):
                more += landed[1, n]
            total[...] += more[:, :seqs]

        if pushed:
            when(outer, add_more)

    def drain():
        def columns(half, first, count):
            lanes = half * half_lanes + first * part_lanes
            return out.at[:, pl.ds(pl.multiple_of(lanes, part_lanes), count * part_lanes)]

        await_all(columns(1 - x, pushed, quarters - pushed), precv.at[0, 1])
        if pushed:
            await_all(columns(1 - x, 0, pushed), precv.at[0, 0], no(outer))
            for n, half in ((1, x), (2, 1 - x)):
                await_all(columns(half, 0, pushed), precv.at[n, 0], outer)
        sum_scores()
        if planes > 1:
            z_sent()
        for kind, first, count in ((0, 0, pushed), (1, pushed, quarters - pushed)):
            lanes = pl.ds(first * part_lanes, count * part_lanes)
            if count:
                await_sent(picked.at[0, :, lanes], psent.at[0, kind], True if kind else no(outer))
                for n in (1, 2):
                    if not kind:
                        await_sent(picked.at[n, :, lanes], psent.at[n, kind], inner)
        for condition, copy in sent:
            when(condition, copy.wait_send)
        for condition, copy in head_copies():
            when(condition, copy.wait_send)

    share_scores()
    drain()


def body(
    activations,
    out_grads,
    proj_in,
    proj_out,
    left_factor,
    right_factor,
    seq_lengths,
    seq_slots,
    stored_grads,
):
    dma = pltpu.SemaphoreType.DMA
    feats, toks = lax.axis_size("feat"), lax.axis_size("tok")
    rank = right_factor.shape[0]
    tok_rows = activations.shape[0]
    seqs = seq_lengths.shape[0]
    local = seqs // toks
    chunk = tok_rows // local
    store_rows, width = stored_grads.shape
    planes, chips = toks // 2, feats // 2
    wide = rank // feats
    quarters = wide // 16
    tiles = rank // 128
    score_rows = store_rows // feats
    lanes = seqs + -seqs % 128
    half = chunk // 2
    steps = max(planes - 1, 1)
    pieces = width // 2 // (2 * rank)
    pushed = pushed_quarters(planes, quarters)
    aside = max(pushed, 1)
    aside_lanes = aside * 8 * rank

    def vmem(*shape, dtype=F32):
        return pltpu.VMEM(shape, dtype)

    scores, own_rows = pl.pallas_call(
        functools.partial(kernel, (toks, feats, local, chunk, rank, seqs, store_rows)),
        out_shape=[
            pltpu.VMEM((score_rows, seqs), F32),
            pltpu.VMEM((local, width), F32),
        ],
        in_specs=[ANY] * 9,
        out_specs=[VMEM, VMEM],
        scratch_shapes=[
            vmem(*out_grads.shape, dtype=BF16),
            vmem(*activations.shape, dtype=BF16),
            vmem(*proj_out.shape, dtype=BF16),
            vmem(*proj_in.shape, dtype=BF16),
            vmem(rank, rank),
            vmem(rank, rank),
            vmem(1, seqs, dtype=jnp.int32),
            vmem(1, seqs, dtype=jnp.int32),
            vmem(2, rank, rank, dtype=BF16),
            vmem(3 * rank, rank, dtype=BF16),
            vmem(2, *proj_out.shape, dtype=BF16),
            vmem(local, 2, chips, wide, chunk),
            vmem(local, chips, wide, chunk),
            vmem(local, chips, wide, chunk),
            vmem(local, chips - 1, wide, chunk),
            vmem(local, wide, chunk),
            vmem(local, 2, half, rank),
            vmem(local, half, rank),
            vmem(local, half, rank),
            vmem(local, chips - 1, half, rank),
            vmem(local, 2, half, rank),
            vmem(local + 1, 2, quarters, tiles, 8, 128),
            vmem(quarters, tiles, 8, 128),
            vmem(quarters, tiles, 8, 128),
            vmem(quarters, tiles, seqs * 8, 128),
            vmem(store_rows, width // 2),
            vmem(store_rows, width // 2),
            vmem(2, store_rows, aside_lanes),
            vmem(4 * store_rows, width // 2, dtype=BF16),
            vmem(4 * store_rows, aside_lanes, dtype=BF16),
            vmem(planes, 4 * local, 4 * store_rows),
            vmem(planes, 4 * local, 4 * store_rows),
            vmem(3, local, width // 2),
            vmem(2, 2, feats, score_rows, lanes),
            vmem(2, 2 * feats, score_rows, lanes),
            dma((2 * (local // 2 if local % 2 == 0 else local) + 7,)),
            dma((2, local // 2 if local % 2 == 0 else local)),
            dma((2, local, chips - 1)),
            dma((local,)),
            dma((local,)),
            dma((2,)),
            dma((2, local // 2 + 1)),
            dma((2, steps, (local + 1) // 2)),
            dma((2, quarters)),
            dma((8,)),
            dma((3, 2)),
            dma((2,)),
            dma((2,)),
            dma((2, chips - 1)),
            dma((1,)),
            dma((1,)),
            dma((3,)),
            dma((2, 2, steps)),
            dma((4,)),
            dma((3, 2)),
            dma((2,)),
        ],
        compiler_params=pltpu.CompilerParams(
            collective_id=0, has_side_effects=True, vmem_limit_bytes=60 << 20
        ),
        name="influence",
    )(
        out_grads, activations, proj_out, proj_in, left_factor, right_factor,
        seq_lengths.reshape(1, seqs), seq_slots.reshape(1, seqs), stored_grads,
    )
    return scores, own_rows


def solution(mesh):
    placed = (
        P("tok", "feat"),
        P("tok", "feat"),
        P("feat", None),
        P("feat", None),
        P(),
        P(),
        P(),
        P(),
        P("tok", "feat"),
    )
    return jax.shard_map(
        body,
        mesh=mesh,
        in_specs=placed,
        out_specs=(P(("tok", "feat"), None), P("tok", "feat")),
        check_vma=False,
    )
```

```python
import functools

import jax
import jax.numpy as jnp
from jax import lax
from jax.experimental import pallas as pl
from jax.experimental.pallas import tpu as pltpu
from jax.sharding import PartitionSpec as P

MESH = pl.DeviceIdType.MESH
VMEM = pl.BlockSpec(memory_space=pltpu.VMEM)
ANY = pl.BlockSpec(memory_space=pl.ANY)
F32, BF16 = jnp.float32, jnp.bfloat16
DOWN, UP = 0, 1


def halves(value):
    high = value.astype(BF16)
    return high, (value - high.astype(F32)).astype(BF16)


def times(left, right):
    return jnp.dot(left, right, preferred_element_type=F32)


def times_t(left, right):
    return lax.dot_general(left, right, (((1,), (1,)), ((), ())), preferred_element_type=F32)


def stack_left(value, axis):
    high, low = halves(value)
    return jnp.concatenate([high, low, high], axis=axis)


def stack_right(value, axis):
    high, low = halves(value)
    return jnp.concatenate([high, high, low], axis=axis)


def aligned(index, size):
    return pl.ds(pl.multiple_of(index * size, size), size)


def pushed_quarters(planes, quarters):
    return quarters // 2 if planes == 4 else 0


def both(first, second):
    if first is True:
        return second
    if second is True:
        return first
    return False if first is False or second is False else first & second


def no(value):
    return not value if isinstance(value, bool) else jnp.logical_not(value)


def when(condition, action):
    if condition is True:
        action()
    elif condition is not False:
        pl.when(condition)(action)


def kernel(dims, *refs):
    toks, feats, local, chunk, rank, seqs, store_rows = dims
    out_rows, in_rows, out_mat, in_mat, left_hbm, right_hbm, lens_hbm, slots_hbm, stored = refs[:9]
    total, out = refs[9:11]
    lhs_o, lhs_i, rhs_o, rhs_i, left_f, right_f, lens, slots = refs[11:19]
    left_cat, right_cat, folded = refs[19:22]
    lp, la, ly, lb, lfin = refs[22:27]
    rp, ra, ry, rb, rfull = refs[27:32]
    block, hx, hz, gs = refs[32:36]
    kept, given, guest, mats, guest_mats, sc, guest_sc = refs[36:43]
    picked, scored, landed = refs[43:46]
    load, asem, bsem, csem, xsem, hsem, zpushed, zkept, zlast, srecv, precv, rrecv = refs[46:58]
    asent, bsent, csent, xsent, hsent, zsent, ssent, psent, rsent = refs[58:]

    tok, feat = lax.axis_index("tok"), lax.axis_index("feat")
    plane, x = tok // 2, tok % 2
    y, c = feat // 2, feat % 2
    planes = toks // 2
    mate, chips = feat + 1 - 2 * c, feats // 2
    across = [(y + turn) % chips for turn in range(1, chips)]
    beside = tok + 1 - 2 * x
    wide = rank // feats
    half_o = wide // 2
    quarters = half_o // 8
    in_plane = 2 * local
    half_lanes = half_o * rank
    part_lanes = 8 * rank
    tiles = rank // 128
    below, above = plane > 0, plane < planes - 1
    pushed = pushed_quarters(planes, quarters)
    outer = inner = False
    if pushed:
        outer = (plane == 0) | (plane == planes - 1)
        inner = (plane == 1) | (plane == planes - 2)
    partner = jnp.where(plane == 0, 1, jnp.where(
        plane == planes - 1, planes - 2, jnp.where(plane == 1, 0, planes - 1)))

    def remote(src, dst, sems, to_tok, to_feat):
        return pltpu.make_async_remote_copy(
            src_ref=src, dst_ref=dst, send_sem=sems[0], recv_sem=sems[1],
            device_id=(to_tok, to_feat), device_id_type=MESH,
        )

    loads = {}
    span = 2 if local % 2 == 0 else 1
    blocks = local // span
    tall = span * chunk

    def fetch(key, src, dst):
        loads[key] = pltpu.make_async_copy(src, dst, load.at[len(loads)])
        loads[key].start()

    def fetch_block(b):
        if b < blocks:
            rows = pl.ds(b * tall, tall)
            if b:
                fetch(("o", b), out_rows.at[rows], lhs_o.at[rows])
            fetch(("i", b), in_rows.at[rows], lhs_i.at[rows])

    fetch("left", left_hbm, left_f)
    fetch("out", out_mat, rhs_o)
    fetch(("o", 0), out_rows.at[pl.ds(0, tall)], lhs_o.at[pl.ds(0, tall)])
    fetch("in", in_mat, rhs_i)
    fetch_block(0)
    fetch("lens", lens_hbm, lens)
    fetch("slots", slots_hbm, slots)
    fetch("right", right_hbm, right_f)

    barrier = pltpu.get_barrier_semaphore()

    def greet(to_tok, to_feat):
        pl.semaphore_signal(barrier, inc=1, device_id=(to_tok, to_feat), device_id_type=MESH)

    for step in range(2):
        for turn in range(feats):
            if step or turn:
                greet(beside if step else tok, (feat + turn) % feats)
    met = 2 * feats - 1
    for side, there, crossing in ((-1, below, 0), (1, above, 1)):
        near = False
        if pushed:
            near = (outer & (partner == plane + side)) | (inner & (partner == plane + side))
        plain = both(there, no(near))
        corner = both(plain, x == crossing)
        met += plain.astype(jnp.int32) + corner.astype(jnp.int32)

        def greet_all(side=side):
            for other in range(2):
                for f in range(feats):
                    greet((plane + side) * 2 + other, f)

        if pushed:
            met += 2 * feats * near.astype(jnp.int32)
        when(near, greet_all)
        when(plain, lambda side=side: greet(tok + 2 * side, feat))
        when(corner, lambda side=side: greet(tok + side, feat))

    sent = []

    def start(copy, condition=True):
        when(condition, copy.start)
        return copy

    def await_sent(src, sem, condition=True):
        copy = remote(src, src, (sem, sem), tok, mate)
        sent.append((condition, copy))

    def await_all(dst, sem, condition=True):
        copy = remote(dst, dst, (sem, sem), tok, mate)
        when(condition, copy.wait_recv)

    piece = 2 * rank
    pieces = half_lanes // piece
    aside = pushed * part_lanes // piece
    trades = []

    def column(half, first, count=1):
        lanes = half * half_lanes + first * piece
        return pl.ds(pl.multiple_of(lanes, piece), piece * count)

    def push_own():
        copy = remote(
            stored.at[:, column(x, 0, aside)], guest.at[0], (ssent.at[2], srecv.at[2]),
            partner * 2 + x, feat)
        start(copy, outer)
        await_sent(stored.at[:, column(x, 0, aside)], ssent.at[2], outer)

    batches = 4 if pushed else 0
    batch = aside // 4

    def batch_lanes(n):
        return pl.ds(n * batch * piece, batch * piece)

    def push_given(n):
        lanes = batch_lanes(n)
        await_all(given.at[:, lanes], srecv.at[4 + n], outer)
        start(remote(
            given.at[:, lanes], guest.at[1, :, lanes], (ssent.at[3], srecv.at[3]),
            partner * 2 + x, feat), outer)

    def trade(count):
        for _ in range(count):
            n = len(trades)
            if n < pieces:
                kind = 0 if n < aside else 1
                trades.append(start(remote(
                    stored.at[:, column(1 - x, n)], given.at[:, pl.ds(n * piece, piece)],
                    (ssent.at[kind], srecv.at[1 if kind else 4 + n // batch]), beside, feat,
                )))

    def trades_sent():
        if aside:
            await_sent(stored.at[:, column(1 - x, 0, aside)], ssent.at[0])
            await_sent(given.at[:, pl.ds(0, aside * piece)], ssent.at[3], outer)
        await_sent(stored.at[:, column(1 - x, aside, pieces - aside)], ssent.at[1])

    copies = {}

    def fold_left():
        loads["left"].wait()
        for core in range(2):
            for side in range(chips):
                rows = left_f[pl.ds((side * 2 + core) * wide, wide), :]
                high, low = halves(rows)
                left_cat[0, pl.ds((core * chips + side) * wide, wide), :] = high
                left_cat[1, pl.ds((core * chips + side) * wide, wide), :] = low
        loads["out"].wait()
        depth = rhs_o.shape[0]
        step = min(256, depth)
        for n in range(depth // step):
            rows = rhs_o[pl.ds(n * step, step), :]
            folded[0, pl.ds(n * step, step), :], folded[1, pl.ds(n * step, step), :] = halves(
                times_t(rows, left_cat[0]) + times_t(rows, left_cat[1]))

    def project_out(b):
        loads["o", b].wait()
        own = [lhs_o[pl.ds((b * span + n) * chunk, chunk), :] for n in range(span)]
        sums = [times(rows, folded[0]) + times(rows, folded[1]) for rows in own]
        for n in range(span):
            lp[b * span + n] = jnp.transpose(sums[n]).reshape(2, chips, wide, chunk)

    def send_left(b):
        for k in range(b * span, b * span + span):
            copies["a", 0, k] = start(remote(
                lp.at[k, 1 - c], la.at[k], (asent.at[0], asem.at[0, b]), tok, mate))

    def pair_left(k):
        if k % span == 0:
            await_all(la.at[pl.ds(k, span)], asem.at[0, k // span])
        ly[k] = lp[k, c] + la[k]
        for n, other in enumerate(across):
            copies["b", 0, k, n] = start(remote(
                ly.at[k, other], lb.at[k, n], (bsent.at[0, n], bsem.at[0, k, n]),
                tok, other * 2 + c))

    def project_in(b):
        if b == 0:
            loads["in"].wait()
        loads["i", b].wait()
        if b == 0:
            fetch_block(1)
        fetch_block(b + 2)
        own = [lhs_i[pl.ds((b * span + n) * chunk, chunk), :] for n in range(span)]
        for n, sums in enumerate([times(rows, rhs_i[...]) for rows in own]):
            rp[b * span + n] = sums.reshape(2, chunk // 2, rank)

    def send_right(b):
        for k in range(b * span, b * span + span):
            copies["a", 1, k] = start(remote(
                rp.at[k, 1 - c], ra.at[k], (asent.at[1], asem.at[1, b]), tok, mate))

    def pair_right(k):
        if k % span == 0:
            await_all(ra.at[pl.ds(k, span)], asem.at[1, k // span])
        ry[k] = rp[k, c] + ra[k]
        for n, other in enumerate(across):
            copies["b", 1, k, n] = start(remote(
                ry.at[k], rb.at[k, n], (bsent.at[1, n], bsem.at[1, k, n]),
                tok, other * 2 + c))

    def rows_sent():
        for side, ref in ((0, lp), (1, rp)):
            await_sent(ref.at[:, 1 - c], asent.at[side])
        for n, other in enumerate(across):
            await_sent(ly.at[:, other], bsent.at[0, n])
            await_sent(ry, bsent.at[1, n])
        await_sent(rfull.at[:, c], csent.at[0])
        await_sent(block.at[pl.ds(0, local), 1 - x], xsent.at[0])

    def finish_rows(k):
        if k == 0:
            loads["right"].wait()
            right_cat[...] = stack_right(right_f[...], 0)
        left, rows = ly[k, y], ry[k]
        for n in range(chips - 1):
            copies["b", 0, k, n].wait_recv()
            left += lb[k, n]
        lfin[k] = left
        for n in range(chips - 1):
            copies["b", 1, k, n].wait_recv()
            rows += rb[k, n]
        rfull[k, c] = times(stack_left(rows, 1), right_cat[...])
        copies["c", k] = start(remote(
            rfull.at[k, c], rfull.at[k, c], (csent.at[0], csem.at[k]), tok, mate))

    spans = {}

    def starts_of():
        loads["lens"].wait()
        lengths = lens[...].astype(F32)
        number = lax.broadcasted_iota(jnp.int32, (local, seqs), 1)
        mine = lax.broadcasted_iota(jnp.int32, (local, seqs), 0) + tok * local

        def pick(mask):
            return jnp.sum(jnp.where(mask, lengths, 0.0), axis=1, keepdims=True)

        spans["start"] = pick(number < mine)
        spans["now"] = 1.0 / jnp.maximum(pick(number == mine), 1.0)
        spans["before"] = 1.0 / jnp.maximum(pick(number == mine - 1), 1.0)

    def seq_rows(at_plane, number, side, count=1):
        first = (at_plane * in_plane + number * 2 + side) * 8
        return pl.ds(pl.multiple_of(first, 8), 8 * count)

    def settle(k, value):
        for tile in range(tiles):
            part = value[:, tile * 128 : (tile + 1) * 128]
            block[k, :, :, tile] = part.reshape(2, quarters, 8, 128)
        if k < local:
            gs[:, :, seq_rows(plane, k, x), :] = block[k, x]
            copies["x", k] = start(remote(
                block.at[k, 1 - x], gs.at[:, :, seq_rows(plane, k, x), :],
                (xsent.at[0], xsem.at[k]), beside, feat))
            if k < local - 1:
                z_own(k, x)

    def head_copies():
        return (
            (x == 1, remote(block.at[local, 0], hx, (hsent.at[0], hsem.at[0]), beside, feat)),
            ((x == 0) & below, remote(
                block.at[local, 0], hz, (hsent.at[1], hsem.at[1]), tok - 2, feat)),
            ((x == 0) & below, remote(
                block.at[local, 1], hz, (hsent.at[2], hsem.at[1]), tok - 1, feat)),
        )

    carry = {}

    def gradients(k):
        if k == 0:
            starts_of()
        copies["c", k].wait_recv()
        places = lax.broadcasted_iota(jnp.int32, (1, chunk), 1) + (tok * local + k) * chunk
        inside = places.astype(F32) >= spans["start"][k : k + 1]
        now = jnp.where(inside, spans["now"][k : k + 1], 0.0)
        before = jnp.where(inside, 0.0, spans["before"][k : k + 1])
        left = lfin[k]
        weighted = jnp.concatenate([left * now, left * before], axis=0)
        right = rfull[k].reshape(chunk, rank)
        both = times(stack_left(weighted, 1), stack_right(right, 0))
        tail = both[wide:]
        if k:
            settle(k - 1, carry["sum"] + tail)
        else:
            settle(local, tail)
            for condition, copy in head_copies():
                when(condition, copy.start)
        carry["sum"] = both[:wide]
        if k == local - 1:
            settle(k, carry["sum"])

    ways = (DOWN, UP)

    def block_plane(way, step):
        return jnp.clip(plane + step if way == DOWN else plane - step, 0, planes - 1)

    def to_outer(way):
        return (plane == 1 if way == DOWN else plane == planes - 2) if pushed else False

    def sending(way, step, kind=1):
        if way == DOWN:
            base = below & (plane + step < planes)
        else:
            base = above & (plane - step >= 0)
        return base if kind else both(base, no(to_outer(way)))

    def taking(way, step, kind=1):
        base = plane + 1 + step < planes if way == DOWN else plane - 1 - step >= 0
        return base if kind else both(base, no(outer))

    groups = local // 2
    tail_parts = range(pushed, quarters)
    kinds = (0, 1) if pushed else (1,)

    def z_data(at, kind, first, count):
        which = pl.ds(pushed, quarters - pushed) if kind else pl.ds(0, pushed)
        return gs.at[which, :, seq_rows(at, first, 0, 2 * count), :]

    def z_start(way, step, kind, first, count, part=None):
        data = z_data(block_plane(way, step), kind, first, count)
        came = came_by(way, kind, step, first // 2)
        if part is not None:
            data = gs.at[part, :, seq_rows(block_plane(way, step), first, 0, 2 * count), :]
            came = zlast.at[way, part]
        copy = remote(
            data, data, (zsent.at[way, kind, step], came),
            tok - 2 if way == DOWN else tok + 2, feat)
        when(sending(way, step, kind), copy.start)

    def came_by(way, kind, step, group):
        if kind:
            return zkept.at[way, step, group]
        return zpushed.at[way, groups if step else group]

    def take_pushed():
        for way in ways:
            data = z_data(block_plane(way, 2), 0, 0, local)
            await_all(data, came_by(way, 0, 1, 0), taking(way, 1, 0))

    def z_own(number, side):
        if planes > 1:
            for kind in kinds:
                which = pl.ds(pushed, quarters - pushed) if kind else pl.ds(0, pushed)
                data = gs.at[which, :, seq_rows(plane, number, side), :]
                for way in ways:
                    copy = remote(
                        data, data, (zsent.at[way, kind, 0], came_by(way, kind, 0, number // 2)),
                        tok - 2 if way == DOWN else tok + 2, feat)
                    when(sending(way, 0, kind), copy.start)

    def z_sent():
        for step in range(last_step + 1):
            for way in ways:
                for kind in kinds:
                    if kind or step < 2:
                        data = z_data(block_plane(way, step), kind, 0, local)
                        await_sent(data, zsent.at[way, kind, step], sending(way, step, kind))

    last_step = max(planes - 2, 0)

    def complete(k):
        copies["x", k].wait_recv()
        if k == local - 1:
            @pl.when(x == 1)
            def _():
                gs[:, :, seq_rows(plane, k, 0), :] += block[local, 1]

            @pl.when(x == 0)
            def _():
                head_copies()[0][1].wait_recv()
                gs[:, :, seq_rows(plane, k, 0), :] += hx[...]

            @pl.when(above)
            def _():
                head_copies()[1][1].wait_recv()
                gs[:, :, seq_rows(plane, k, 1), :] += hz[...]
        z_own(k, 1 - x)
        if k == local - 1:
            z_own(k, x)

    def take(step, kind, group):
        for way in ways:
            data = z_data(block_plane(way, step + 1), kind, 2 * group, 2)
            await_all(data, came_by(way, kind, step, group), taking(way, step, kind))

    whole_groups = groups - 1 if last_step >= 2 else groups

    def pass_on(step, group, only=kinds):
        if planes > 1 and step <= last_step:
            for kind in only:
                if kind or step < 2:
                    take(step, kind, group)
                if step < last_step and (kind or step + 1 < 2):
                    split = step + 1 == last_step and last_step >= 2
                    for way in ways:
                        if not split or group < whole_groups:
                            z_start(way, step + 1, kind, 2 * group, 2)
                    if split and group == groups - 1:
                        for part in tail_parts:
                            for way in ways:
                                z_start(way, step + 1, kind, 2 * whole_groups,
                                        local - 2 * whole_groups, part)

    def take_last(part):
        first = 2 * whole_groups
        for way in ways:
            at = block_plane(way, last_step + 1)
            data = gs.at[part, :, seq_rows(at, first, 0, 2 * (local - first)), :]
            await_all(data, zlast.at[way, part], taking(way, last_step))

    def make_mats(target, rows, lanes, value):
        high, low = halves(value)
        count = 2 * store_rows
        target[pl.ds(rows * store_rows, store_rows), lanes] = high
        target[pl.ds(count + rows * store_rows, store_rows), lanes] = low

    def score(target, at, part):
        lines = []
        for line in range(8):
            first = at * in_plane * 8 + line
            for tile in range(tiles):
                lines.append(gs[part, tile, pl.ds(first, in_plane, stride=8), :])
        high, low = halves(jnp.concatenate(lines, axis=1))
        return times_t(
            jnp.concatenate([high, low], axis=0),
            target[:, pl.ds(part * part_lanes, part_lanes)],
        )

    def score_plane(at):
        value = score(mats, at, pushed)
        for part in range(pushed + 1, quarters):
            value += score(mats, at, part)
        sc[at] = value

        def more():
            value = score(mats, at, 0)
            for part in range(1, pushed):
                value += score(mats, at, part)
            sc[at] += value

        if pushed:
            when(no(outer), more)

    def score_guests():
        for step in range(2):
            await_all(guest.at[step], srecv.at[2 + step])
        lanes = pl.ds(0, pushed * part_lanes)
        for step in range(2):
            make_mats(guest_mats, step, lanes, guest[step])
        for at in range(planes):
            value = score(guest_mats, at, 0)
            for part in range(1, pushed):
                value += score(guest_mats, at, part)
            guest_sc[at] = value

    def score_step(step):
        for way in ways:
            when(taking(way, step), lambda way=way: score_plane(block_plane(way, step + 1)))

    def stage_rows(k):
        if 0 <= k < local:
            finish_rows(k)

    def stage_grads(k):
        if 0 <= k < local:
            gradients(k)

    def stage_complete(k):
        if 0 <= k < local:
            complete(k)

    fold_left()
    project_out(0)
    pl.semaphore_wait(barrier, met)
    send_left(0)
    if pushed:
        push_own()
    trade(3)
    early = min(2, local) if blocks >= 3 else 0
    for b in range(blocks):
        chunks = range(b * span, b * span + span)
        if b == 0:
            for k in chunks:
                pair_left(k)
        project_in(b)
        send_right(b)
        if b:
            for k in chunks:
                pair_left(k)
        if b == 1:
            trade(2)
        if b == blocks - 2 and early:
            stage_rows(0)
        if b + 1 < blocks:
            project_out(b + 1)
            send_left(b + 1)
        else:
            fetch("kept", stored.at[:, column(x, 0, pieces)], kept)
            if early:
                stage_grads(1)
        for k in chunks:
            pair_right(k)
        if b == blocks - 2 and early:
            stage_grads(0)
            stage_rows(1)
    passed = 0
    for k in range(early, local):
        stage_rows(k)
        stage_complete(k - 3)
        stage_grads(k)
        if k >= 5 and k % 2 and k < local - 1:
            pass_on(0, (k - 5) // 2)
            passed = (k - 5) // 2 + 1
    trade(pieces)
    trades_sent()
    rows_sent()
    stage_complete(local - 3)
    loads["kept"].wait()
    make_mats(mats, 0, pl.ds(0, half_lanes), kept[...])
    stage_complete(local - 2)
    stage_complete(local - 1)
    for group in range(passed, groups - 2):
        pass_on(0, group)
    passed = max(passed, groups - 2)
    for n in range(batches):
        push_given(n)
    pass_on(1, 0, (1,))

    loads["slots"].wait()
    at_row = lax.broadcasted_iota(jnp.int32, (seqs, seqs), 1)
    seq_of = ((at_row // in_plane) * 2 + at_row % 2) * local + (at_row % in_plane) // 2
    by_seq = jnp.where(lax.broadcasted_iota(jnp.int32, (seqs, seqs), 0) == seq_of, 1.0, 0.0)
    by_seq = by_seq.astype(BF16)
    slot = lax.broadcasted_iota(jnp.int32, (seqs, seqs), 0)
    by_slot = times(
        jnp.where(slots[...] == slot, 1.0, 0.0).astype(BF16), by_seq)
    row = lax.broadcasted_iota(jnp.int32, (4 * local, seqs), 0)
    wanted = jnp.zeros((4 * local, seqs), jnp.int32)
    for n, owner in enumerate((tok, beside, partner * 2 + x, partner * 2 + 1 - x)):
        here = (row >= n * local) & (row < (n + 1) * local)
        wanted = jnp.where(here, owner * local + row - n * local, wanted)
    pick = times(
        jnp.where(slots[...] == wanted, 1.0, 0.0).astype(BF16), by_seq).astype(BF16)
    pick = jnp.concatenate([pick, pick], axis=1)

    for group in range(passed, groups):
        pass_on(0, group)
        pass_on(1, group - 1, (1,))

    def given_mats(first, count):
        lanes = pl.ds(first * part_lanes, count * part_lanes)
        make_mats(mats, 1, lanes, given[:, lanes])

    def give(part, n, to, condition):
        lane = part * part_lanes
        there = pl.ds(pl.multiple_of(x * half_lanes + lane, part_lanes), part_lanes)
        sem = psent.at[n, 0 if part < pushed else 1]
        copies["p", n, part] = start(remote(
            picked.at[n, :, pl.ds(lane, part_lanes)], out.at[:, there],
            (sem, precv.at[n, 0 if part < pushed else 1]), to, feat), condition)

    def fill_rows(part):
        count = 4 if part < pushed else 2
        for line in range(8):
            high, low = halves(jnp.concatenate(
                [gs[part, tile, pl.ds(line, seqs, stride=8), :] for tile in range(tiles)], axis=1))
            taken = times(pick[: count * local], jnp.concatenate([high, low], axis=0))
            lane = part * part_lanes + line * rank
            out[:, pl.ds(pl.multiple_of(x * half_lanes + lane, rank), rank)] = taken[:local]
            for n in range(1, count):
                picked[n - 1, :, pl.ds(lane, rank)] = taken[n * local : (n + 1) * local]

    def hand_rows(part, condition):
        if part < pushed:
            give(part, 2, partner * 2 + 1 - x, inner)
            give(part, 1, partner * 2 + x, inner)
        give(part, 0, beside, condition)

    def rows_for_slots(part):
        condition = no(outer) if part < pushed else True
        when(condition, lambda: fill_rows(part))
        hand_rows(part, condition)

    def turn_scores(sums):
        count = 2 * store_rows
        high, low = sums[:, :in_plane], sums[:, in_plane:]
        by_row = (high[:, :, :count] + high[:, :, count:] + low[:, :, :count]).reshape(seqs, count)
        lanes = scored.shape[4]
        placed = jnp.dot(
            by_slot, by_row, precision=lax.Precision.HIGHEST, preferred_element_type=F32)
        if lanes > seqs:
            placed = jnp.concatenate([placed, jnp.zeros((lanes - seqs, count), F32)], axis=0)
        return jnp.transpose(
            jnp.concatenate([placed, jnp.zeros((lanes, 128 - count), F32)], axis=1))

    few = scored.shape[3]
    parts = {}

    def send_scores(kind, own, condition):
        base = partner if kind else plane
        for step in range(2):
            for turn in range(feats):
                if kind or step or turn:
                    to = (feat + turn) % feats
                    parts[kind, step, turn] = start(remote(
                        scored.at[kind, step, to], landed.at[kind, step * feats + turn],
                        (rsent.at[kind], rrecv.at[kind]),
                        base * 2 + (1 - x if step else x), to,
                    ), condition)
        first = 0 if kind else 1
        await_sent(landed.at[kind, pl.ds(first, 2 * feats - first)], rsent.at[kind], condition)

    def place_scores(kind, sums):
        turned = turn_scores(sums)
        for step in range(2):
            for f in range(feats):
                first = (step * feats + f) * few
                scored[kind, step, f] = turned[first : first + few]

    def share_guests():
        when(inner, lambda: place_scores(1, guest_sc[...]))
        send_scores(1, guest_sc, inner)

    def share_scores():
        place_scores(0, sc[...])
        send_scores(0, sc, True)

    if pushed:
        take_pushed()
        pass_on(1, groups - 1, (1,))
        for part in range(pushed):
            rows_for_slots(part)
        when(inner, score_guests)
        share_guests()
        when(inner, lambda: [fill_rows(part) for part in tail_parts] and None)
        for part in tail_parts:
            hand_rows(part, inner)
    else:
        pass_on(1, groups - 1, (1,))
    for n in range(batches):
        await_all(given.at[:, batch_lanes(n)], srecv.at[4 + n], no(outer))
    await_all(given.at[:, pl.ds(aside * piece, (pieces - aside) * piece)], srecv.at[1])
    given_mats(pushed, quarters - pushed)
    if pushed:
        when(no(outer), lambda: given_mats(0, pushed))
    score_plane(plane)
    score_step(0)
    if last_step > 0:
        score_step(1)
    for step in range(2, last_step + 1):
        for group in range(groups if step < last_step else whole_groups):
            pass_on(step, group)
        if step < last_step:
            score_step(step)
    for part in tail_parts:
        if last_step >= 2:
            take_last(part)
        if pushed:
            when(outer, lambda part=part: fill_rows(part))
            hand_rows(part, outer)
        else:
            rows_for_slots(part)
    if last_step >= 2:
        score_step(last_step)

    def sum_scores():
        others = pl.ds(1, 2 * feats - 1)
        await_all(landed.at[0, others], rrecv.at[0])
        summed = scored[0, 0, feat]
        for n in range(1, 2 * feats):
            summed += landed[0, n]
        total[...] = summed[:, :seqs]

        def add_more():
            await_all(landed.at[1], rrecv.at[1])
            more = landed[1, 0]
            for n in range(1, 2 * feats):
                more += landed[1, n]
            total[...] += more[:, :seqs]

        if pushed:
            when(outer, add_more)

    def drain():
        def columns(half, first, count):
            lanes = half * half_lanes + first * part_lanes
            return out.at[:, pl.ds(pl.multiple_of(lanes, part_lanes), count * part_lanes)]

        await_all(columns(1 - x, pushed, quarters - pushed), precv.at[0, 1])
        if pushed:
            await_all(columns(1 - x, 0, pushed), precv.at[0, 0], no(outer))
            for n, half in ((1, x), (2, 1 - x)):
                await_all(columns(half, 0, pushed), precv.at[n, 0], outer)
        sum_scores()
        if planes > 1:
            z_sent()
        for kind, first, count in ((0, 0, pushed), (1, pushed, quarters - pushed)):
            lanes = pl.ds(first * part_lanes, count * part_lanes)
            if count:
                await_sent(picked.at[0, :, lanes], psent.at[0, kind], True if kind else no(outer))
                for n in (1, 2):
                    if not kind:
                        await_sent(picked.at[n, :, lanes], psent.at[n, kind], inner)
        for condition, copy in sent:
            when(condition, copy.wait_send)
        for condition, copy in head_copies():
            when(condition, copy.wait_send)

    share_scores()
    drain()


def body(
    activations,
    out_grads,
    proj_in,
    proj_out,
    left_factor,
    right_factor,
    seq_lengths,
    seq_slots,
    stored_grads,
):
    dma = pltpu.SemaphoreType.DMA
    feats, toks = lax.axis_size("feat"), lax.axis_size("tok")
    rank = right_factor.shape[0]
    tok_rows = activations.shape[0]
    seqs = seq_lengths.shape[0]
    local = seqs // toks
    chunk = tok_rows // local
    store_rows, width = stored_grads.shape
    planes, chips = toks // 2, feats // 2
    wide = rank // feats
    quarters = wide // 16
    tiles = rank // 128
    score_rows = store_rows // feats
    lanes = seqs + -seqs % 128
    half = chunk // 2
    steps = max(planes - 1, 1)
    pieces = width // 2 // (2 * rank)
    pushed = pushed_quarters(planes, quarters)
    aside = max(pushed, 1)
    aside_lanes = aside * 8 * rank

    def vmem(*shape, dtype=F32):
        return pltpu.VMEM(shape, dtype)

    scores, own_rows = pl.pallas_call(
        functools.partial(kernel, (toks, feats, local, chunk, rank, seqs, store_rows)),
        out_shape=[
            pltpu.VMEM((score_rows, seqs), F32),
            pltpu.VMEM((local, width), F32),
        ],
        in_specs=[ANY] * 9,
        out_specs=[VMEM, VMEM],
        scratch_shapes=[
            vmem(*out_grads.shape, dtype=BF16),
            vmem(*activations.shape, dtype=BF16),
            vmem(*proj_out.shape, dtype=BF16),
            vmem(*proj_in.shape, dtype=BF16),
            vmem(rank, rank),
            vmem(rank, rank),
            vmem(1, seqs, dtype=jnp.int32),
            vmem(1, seqs, dtype=jnp.int32),
            vmem(2, rank, rank, dtype=BF16),
            vmem(3 * rank, rank, dtype=BF16),
            vmem(2, *proj_out.shape, dtype=BF16),
            vmem(local, 2, chips, wide, chunk),
            vmem(local, chips, wide, chunk),
            vmem(local, chips, wide, chunk),
            vmem(local, chips - 1, wide, chunk),
            vmem(local, wide, chunk),
            vmem(local, 2, half, rank),
            vmem(local, half, rank),
            vmem(local, half, rank),
            vmem(local, chips - 1, half, rank),
            vmem(local, 2, half, rank),
            vmem(local + 1, 2, quarters, tiles, 8, 128),
            vmem(quarters, tiles, 8, 128),
            vmem(quarters, tiles, 8, 128),
            vmem(quarters, tiles, seqs * 8, 128),
            vmem(store_rows, width // 2),
            vmem(store_rows, width // 2),
            vmem(2, store_rows, aside_lanes),
            vmem(4 * store_rows, width // 2, dtype=BF16),
            vmem(4 * store_rows, aside_lanes, dtype=BF16),
            vmem(planes, 4 * local, 4 * store_rows),
            vmem(planes, 4 * local, 4 * store_rows),
            vmem(3, local, width // 2),
            vmem(2, 2, feats, score_rows, lanes),
            vmem(2, 2 * feats, score_rows, lanes),
            dma((2 * (local // 2 if local % 2 == 0 else local) + 7,)),
            dma((2, local // 2 if local % 2 == 0 else local)),
            dma((2, local, chips - 1)),
            dma((local,)),
            dma((local,)),
            dma((2,)),
            dma((2, local // 2 + 1)),
            dma((2, steps, (local + 1) // 2)),
            dma((2, quarters)),
            dma((8,)),
            dma((3, 2)),
            dma((2,)),
            dma((2,)),
            dma((2, chips - 1)),
            dma((1,)),
            dma((1,)),
            dma((3,)),
            dma((2, 2, steps)),
            dma((4,)),
            dma((3, 2)),
            dma((2,)),
        ],
        compiler_params=pltpu.CompilerParams(
            collective_id=0, has_side_effects=True, vmem_limit_bytes=60 << 20
        ),
        name="influence",
    )(
        out_grads, activations, proj_out, proj_in, left_factor, right_factor,
        seq_lengths.reshape(1, seqs), seq_slots.reshape(1, seqs), stored_grads,
    )
    return scores, own_rows


def solution(mesh):
    placed = (
        P("tok", "feat"),
        P("tok", "feat"),
        P("feat", None),
        P("feat", None),
        P(),
        P(),
        P(),
        P(),
        P("tok", "feat"),
    )
    return jax.shard_map(
        body,
        mesh=mesh,
        in_specs=placed,
        out_specs=(P(("tok", "feat"), None), P("tok", "feat")),
        check_vma=False,
    )
```
